512 devices in a mesh: grp: 64 (over z, y), seq: 8 (over x, core).
Axes of the slice: x: 4, y: 4, z: 16, core: 2. Of those that a mesh axis runs over, the one named last changes fastest.
Arguments:
- tokens: bfloat16 [64, 1024, 2048], P('grp', 'seq'), may hold values from -6 to 6
- seg_ids: int32 [64, 1024], P('grp'), may hold values from 0 to 3, never falling along the last dimension, each value on 1 to 512 neighbouring positions
- deal: int32 [64, 1024], P('grp'), may hold values from 0 to 1023, each once within a row
- page_table: int32 [64, 128], P('grp'), may hold values from 0 to 127, each once within a row
- in_gain: float32 [2048], replicated, may hold values from 0.1 to 1.9
- w_query: bfloat16 [2048, 2048], P('grp', 'seq'), may hold values from -0.125 to 0.125
- key_projection_weight: bfloat16 [2048, 512], P('grp'), may hold values from -0.125 to 0.125
- value_projection_weight: bfloat16 [2048, 512], P('grp'), may hold values from -0.125 to 0.125
- q_gain: float32 [256], replicated, may hold values from 1.25 to 3.75
- key_norm_gain: float32 [256], replicated, may hold values from 0.1 to 1.9
- w_out: bfloat16 [2048, 2048], P('seq', 'grp'), may hold values from -0.125 to 0.125
- post_gain: float32 [2048], replicated, may hold values from 0.1 to 1.9
- final_gain: float32 [2048], replicated, may hold values from 0.1 to 1.9
- embed: bfloat16 [262144, 2048], P(('grp', 'seq')), may hold values from -0.375 to 0.375
Outputs:
- hidden_out: bfloat16 [64, 1024, 2048], P('grp', 'seq')
- kv_cache: bfloat16 [64, 128, 8, 1024], P('grp', 'seq')
- last_norm: float32 [256], replicated
- max_logit: float32 [256], replicated
The draws below stay inside these ranges and needn't reach their ends.
Inputs may be any that keep to these rules, and one draw needn't show every extreme that they name: `seg_ids`: along each pack the prompt numbers never fall; every one of the 4 prompts occurs, none has more than 512 positions, and one has exactly that many. Each row of deal holds every packed position once. Each row of page_table holds every page of the pack once.
All inputs are finite; a program needn't handle non-finite values.
Results may differ from the reference program's by a relative error of at most 0.015.
The reference program's roundings to bfloat16 on the way count: a program that leaves them out, or rounds other values in their place, can miss the bound.
Values may be sent and summed in bfloat16 or wider, within the bound.
A program may use at most 64 MiB of HBM per device.

```python
import math
import jax
import jax.numpy as jnp
import numpy as np
from jax import lax

MODEL_WIDTH = 2048
QUERY_HEADS = 8
KEY_HEADS = 2
HEAD_SIZE = 256
VOCAB = 262144
PAGE_SLOTS = 8
SEGS = 4
PACK_TOKENS = 1024
PACK_PAGES = 128
GROUPS = 64
REQS = 256
N_GRP = 64
N_SEQ = 8


def draw_q_gain(key, part):
    amplitude = 40.0 / HEAD_SIZE ** 0.5
    factor = jax.random.uniform(key, (HEAD_SIZE,), jnp.float32, 0.5, 1.5)
    return (amplitude * factor).astype(jnp.float32)


def shard_levels(key, extent, pieces, least, top_value):
    def one(position, blocks):
        draws = jax.random.uniform(jax.random.fold_in(jax.random.fold_in(key, 6), position), (blocks,), jnp.float32, least / len(pieces), top_value / len(pieces))
        return jnp.repeat(jnp.exp(draws), extent[position] // blocks).reshape((-1,) + (1,) * (len(extent) - position - 1))

    level = one(*pieces[0])
    for cut in pieces[1:]:
        level = level * one(*cut)
    return level


def profile(number_of, total, reach, skew):
    loads = [(1 << 20) // math.isqrt(rank ** skew) + 1 for rank in range(2, number_of + 1)]
    surplus, given = total - reach - (number_of - 1), [1] * (number_of - 1)
    while surplus > 0:
        movable = [i for i in range(number_of - 1) if given[i] < reach]
        pool, budget = sum([loads[i] for i in movable]), surplus
        for i in movable:
            extra = min(reach - given[i], max(1, budget * loads[i] // pool), surplus)
            given[i] = given[i] + extra
            surplus = surplus - extra
    return np.array([reach] + given)


def ragged_sizes(key, count, total, limit, lean):
    if count == 2:
        one = jax.random.randint(key, (), max(1, total - limit), min(limit, total - 1) + 1)
        return jnp.stack([one, total - one])
    lengths = jnp.asarray(profile(count, total, limit, lean), jnp.int32)
    twos = (count - 1) // 2
    source_of, taker = lengths[1:1 + 2 * twos:2], lengths[2:2 + 2 * twos:2]
    margin = jnp.minimum(source_of - 1, limit - taker)
    shifted = jax.random.randint(jax.random.fold_in(key, 1), (twos,), 0, 1 << 20) % (margin + 1)
    lengths = lengths.at[1:1 + 2 * twos:2].set(source_of - shifted).at[2:2 + 2 * twos:2].set(taker + shifted)
    return lengths[jax.random.permutation(jax.random.fold_in(key, 2), count)]


def noise(key, shape, spread, limit, cuts=(), kind=jnp.bfloat16):
    result = jax.random.normal(key, shape, jnp.float32) * spread
    if len(cuts) > 0:
        result = shard_levels(key, shape, cuts, -0.22, 0.18) * result
    return jnp.clip(result, min=-limit, max=limit).astype(kind)


def setup_inputs(seed: int = 0) -> dict:
    arg_keys = jax.random.split(jax.random.key(seed), 15)
    return {
        "tokens": noise(arg_keys[0], (GROUPS, PACK_TOKENS, MODEL_WIDTH), 1.0, 6.0, ((0, 64), (1, 8))),
        "seg_ids": jax.vmap(lambda own: jnp.searchsorted(jnp.cumsum(ragged_sizes(own, SEGS, PACK_TOKENS, PACK_TOKENS // 2, 0)), jnp.arange(PACK_TOKENS), side="right"))(jax.random.split(arg_keys[1], GROUPS)).reshape((GROUPS, PACK_TOKENS)).astype(jnp.int32),
        "deal": jax.vmap(lambda own: jax.random.permutation(own, PACK_TOKENS))(jax.random.split(arg_keys[2], GROUPS)).reshape((GROUPS, PACK_TOKENS)).astype(jnp.int32),
        "page_table": jax.vmap(lambda own: jax.random.permutation(own, PACK_PAGES))(jax.random.split(arg_keys[3], GROUPS)).reshape((GROUPS, PACK_PAGES)).astype(jnp.int32),
        "in_gain": jnp.clip(1.0 + 0.18 * jax.random.normal(arg_keys[4], (MODEL_WIDTH,), jnp.float32), 0.1, 1.9),
        "w_query": noise(arg_keys[5], (MODEL_WIDTH, QUERY_HEADS * HEAD_SIZE), MODEL_WIDTH ** -0.5, 0.125, ((0, 64), (1, 8))),
        "key_projection_weight": noise(arg_keys[6], (MODEL_WIDTH, KEY_HEADS * HEAD_SIZE), MODEL_WIDTH ** -0.5, 0.125, ((0, 64),)),
        "value_projection_weight": noise(arg_keys[7], (MODEL_WIDTH, KEY_HEADS * HEAD_SIZE), MODEL_WIDTH ** -0.5, 0.125, ((0, 64),)),
        "q_gain": draw_q_gain(jax.random.fold_in(arg_keys[14], 71), 0),
        "key_norm_gain": jnp.clip(1.0 + 0.18 * jax.random.normal(arg_keys[9], (HEAD_SIZE,), jnp.float32), 0.1, 1.9),
        "w_out": noise(arg_keys[10], (QUERY_HEADS * HEAD_SIZE, MODEL_WIDTH), (QUERY_HEADS * HEAD_SIZE) ** -0.5, 0.125, ((0, 8), (1, 64))),
        "post_gain": jnp.clip(1.0 + 0.18 * jax.random.normal(arg_keys[11], (MODEL_WIDTH,), jnp.float32), 0.1, 1.9),
        "final_gain": jnp.clip(1.0 + 0.18 * jax.random.normal(arg_keys[12], (MODEL_WIDTH,), jnp.float32), 0.1, 1.9),
        "embed": noise(arg_keys[13], (VOCAB, MODEL_WIDTH), (MODEL_WIDTH // 9) ** -0.5, 0.375, ((0, 512),)),
    }


eps = 1e-06
rope_base = 1000000.0
cap_value = 30.0

def rows_scaled(value_rows, scales):
    mean_square = lax.optimization_barrier(jnp.mean(value_rows * value_rows, axis=-1, keepdims=True))
    return value_rows * lax.rsqrt(mean_square + eps) * scales

def rotate(value_rows, offsets):
    half_width = value_rows.shape[-1] // 2
    frequency = rope_base ** (-2.0 * jnp.arange(half_width, dtype=jnp.float32) / value_rows.shape[-1])
    angles = offsets.astype(jnp.float32)[:, None] * frequency[None, :]
    cosine = jnp.cos(angles)[:, None, :]
    sine_table = jnp.sin(angles)[:, None, :]
    lower_half = value_rows[..., :half_width]
    upper_half = value_rows[..., half_width:]
    return jnp.concatenate([lower_half * cosine - upper_half * sine_table, upper_half * cosine + lower_half * sine_table], axis=-1)

def layout(segment, dealing):
    row_seg = jnp.take(segment, dealing)
    before = lax.optimization_barrier(jnp.sum((segment[None, :] < row_seg[:, None]).astype(jnp.int32), axis=1))
    return (row_seg, (dealing - before).astype(jnp.int32))

def reference(tokens, seg_ids, deal, page_table, in_gain, w_query, key_projection_weight, value_projection_weight, q_gain, key_norm_gain, w_out, post_gain, final_gain, embed):
    query_group_count = QUERY_HEADS // KEY_HEADS
    block_width = QUERY_HEADS * HEAD_SIZE // N_SEQ

    def one_group(packed_in):
        inputs, segment, dealing, page_order = packed_in
        row_seg, offsets = layout(segment, dealing)
        normed_rows = rows_scaled(inputs.astype(jnp.float32), in_gain).astype(jnp.bfloat16)
        query = jnp.dot(normed_rows, w_query, preferred_element_type=jnp.float32).reshape(PACK_TOKENS, QUERY_HEADS, HEAD_SIZE)
        query = rotate(rows_scaled(query, q_gain), offsets).astype(jnp.bfloat16)
        key_rows = jnp.dot(normed_rows, key_projection_weight, preferred_element_type=jnp.float32).reshape(PACK_TOKENS, KEY_HEADS, HEAD_SIZE)
        key_rows = rotate(rows_scaled(key_rows, key_norm_gain), offsets).astype(jnp.bfloat16)
        value_rows = jnp.dot(normed_rows, value_projection_weight, preferred_element_type=jnp.float32).reshape(PACK_TOKENS, KEY_HEADS, HEAD_SIZE)
        value_rows = rows_scaled(value_rows, 1.0).astype(jnp.bfloat16)
        key_rep = jnp.repeat(key_rows, query_group_count, axis=1).astype(jnp.float32)
        value_rep = jnp.repeat(value_rows, query_group_count, axis=1).astype(jnp.float32)
        scores = jnp.einsum('qhd,khd->hqk', query.astype(jnp.float32), key_rep)
        allowed = (row_seg[:, None] == row_seg[None, :]) & (dealing[None, :] <= dealing[:, None])
        masked = jnp.where(allowed[None], scores, -1e+30)
        row_peak = lax.optimization_barrier(jnp.max(masked, axis=-1, keepdims=True))
        raw_weights = jnp.where(allowed[None], jnp.exp(masked - row_peak), 0.0)
        row_total = lax.optimization_barrier(jnp.sum(raw_weights, axis=-1, keepdims=True))
        weights = (raw_weights / row_total).astype(jnp.bfloat16)
        attended = jnp.einsum('hqk,khd->qhd', weights.astype(jnp.float32), value_rep)
        attended = attended.astype(jnp.bfloat16).reshape(PACK_TOKENS, N_SEQ, block_width)
        out_blocks = w_out.reshape(N_SEQ, block_width, MODEL_WIDTH)

        def block_part(index):
            block_in = lax.dynamic_index_in_dim(attended, index, 1, keepdims=False)
            block_w = lax.dynamic_index_in_dim(out_blocks, index, 0, keepdims=False)
            return jnp.dot(block_in, block_w, preferred_element_type=jnp.float32).astype(jnp.bfloat16)
        parts = lax.map(block_part, jnp.arange(N_SEQ, dtype=jnp.int32))
        summed = lax.optimization_barrier(jnp.sum(parts.astype(jnp.float32), axis=0))
        hidden = (inputs.astype(jnp.float32) + rows_scaled(summed, post_gain)).astype(jnp.bfloat16)
        inverse_assignment = jnp.argsort(dealing).astype(jnp.int32)
        stacked_rows = jnp.concatenate([key_rows.reshape(PACK_TOKENS, KEY_HEADS * HEAD_SIZE), value_rows.reshape(PACK_TOKENS, KEY_HEADS * HEAD_SIZE)], axis=1)
        logical_index = jnp.take(stacked_rows, inverse_assignment, axis=0).reshape(PACK_PAGES, PAGE_SLOTS, 2 * KEY_HEADS * HEAD_SIZE)
        cache_pages = jnp.take(logical_index, jnp.argsort(page_order).astype(jnp.int32), axis=0)
        last_pos = lax.optimization_barrier(jnp.sum((segment[None, :] <= jnp.arange(SEGS, dtype=jnp.int32)[:, None]).astype(jnp.int32), axis=1)) - 1
        states = jnp.take(hidden, jnp.take(inverse_assignment, last_pos), axis=0)
        return (hidden, cache_pages, states)
    hidden, cache_pages, states = lax.map(one_group, (tokens, seg_ids, deal, page_table))
    states = states.reshape(REQS, MODEL_WIDTH).astype(jnp.float32)
    last_norm = jnp.sqrt(lax.optimization_barrier(jnp.mean(states * states, axis=-1)))
    final = rows_scaled(states, final_gain).astype(jnp.bfloat16)
    shards = embed.reshape(N_GRP * N_SEQ, VOCAB // (N_GRP * N_SEQ), MODEL_WIDTH)

    def shard_max(block):
        logits = lax.dot_general(final, block, (((1,), (1,)), ((), ())), preferred_element_type=jnp.float32)
        return lax.optimization_barrier(jnp.max(cap_value * jnp.tanh(logits / cap_value), axis=1))
    max_logit = lax.optimization_barrier(jnp.max(lax.map(shard_max, shards), axis=0))
    return (hidden, cache_pages, last_norm, max_logit)
```

```python
import functools

import jax
import jax.numpy as jnp
from jax import lax
from jax.experimental import pallas as pl
from jax.experimental.pallas import tpu as pltpu
from jax.sharding import PartitionSpec as P

MESH = pl.DeviceIdType.MESH
ANY = pl.BlockSpec(memory_space=pl.ANY)
VMEM = pl.BlockSpec(memory_space=pltpu.VMEM)
BF16 = jnp.bfloat16
F32 = jnp.float32
DMA = pltpu.SemaphoreType.DMA

KEY_HEADS = 2
SEGS = 4
NY = 4
NX = 4
NS = 8
CHUNKS = 4
eps = 1e-06
rope_base = 1000000.0
cap_value = 30.0


def remote(src, dst, send_sem, recv_sem, device):
    return pltpu.make_async_remote_copy(
        src_ref=src,
        dst_ref=dst,
        send_sem=send_sem,
        recv_sem=recv_sem,
        device_id=device,
        device_id_type=MESH,
    )


class Place:
    def __init__(self, nz):
        self.nz = nz
        self.g = lax.axis_index("grp")
        self.s = lax.axis_index("seq")
        self.z, self.y = self.g // NY, self.g % NY
        self.x, self.c = self.s // 2, self.s % 2
        self.sib = {"seq": 2 * self.x + 1 - self.c}

    def zn(self, d):
        return {"grp": ((self.z + d + self.nz) % self.nz) * NY + self.y}

    def yn(self, d):
        return {"grp": self.z * NY + (self.y + d + NY) % NY}

    def xs(self, d):
        return 2 * ((self.x + d + NX) % NX) + self.c

    def xn(self, d):
        return {"seq": self.xs(d)}

    def sn(self, d):
        return {"seq": (self.s + d) % NS}


class Link:
    def __init__(self, place):
        self.place = place
        self.sent = []

    def send(self, src, dst, send_sem, recv_sem, device):
        copy = remote(src, dst, send_sem, recv_sem, device)
        copy.start()
        self.sent.append(copy)

    def arrived(self, dst, send_sem, recv_sem):
        remote(dst, dst, send_sem, recv_sem, self.place.sib).wait_recv()

    def finish(self):
        for copy in self.sent:
            copy.wait_send()


def barrier(devices):
    sem = pltpu.get_barrier_semaphore()
    for device in devices:
        pl.semaphore_signal(sem, inc=1, device_id=device, device_id_type=MESH)
    pl.semaphore_wait(sem, len(devices))


def slots(place, k):
    nz = place.nz
    half = nz // 2
    if k == 0:
        return [(0, place.z, 1)]
    if k > half:
        return []
    up = (k, (place.z - k + nz) % nz, 1)
    if k == half:
        return [up]
    return [up, (half + k, (place.z + k) % nz, -1)]


def gather_rows(place, link, own, every, ss, rs):
    step = own.shape[0] // CHUNKS
    piece = lambda s, j: every.at[s, pl.ds(j * step, step)]
    s, left, right, far = place.s, place.xs(-1), place.xs(1), place.xs(2)
    for j in range(CHUNKS):
        mine = own.at[pl.ds(j * step, step)]
        link.send(mine, piece(s, j), ss.at[0, j], rs.at[s, j], place.xn(1))
        link.send(mine, piece(s, j), ss.at[1, j], rs.at[s, j], place.xn(-1))
        link.send(mine, piece(s, j), ss.at[2, j], rs.at[s, j], place.sib)
    keep = pltpu.make_async_copy(own, every.at[s], ss.at[7, 0])
    keep.start()
    yield
    for j in range(CHUNKS):
        link.arrived(piece(left, j), ss.at[0, 0], rs.at[left, j])
        if 2 * j < CHUNKS:
            link.send(piece(left, j), piece(left, j), ss.at[3, j], rs.at[left, j], place.xn(1))
        link.send(piece(left, j), piece(left, j), ss.at[4, j], rs.at[left, j], place.sib)
        link.arrived(piece(right, j), ss.at[0, 0], rs.at[right, j])
        if 2 * j >= CHUNKS:
            link.send(piece(right, j), piece(right, j), ss.at[3, j], rs.at[right, j], place.xn(-1))
        link.send(piece(right, j), piece(right, j), ss.at[5, j], rs.at[right, j], place.sib)
        yield
    for j in range(CHUNKS):
        link.arrived(piece(far, j), ss.at[0, 0], rs.at[far, j])
        link.send(piece(far, j), piece(far, j), ss.at[6, j], rs.at[far, j], place.sib)
        yield
    for x in range(NX):
        other = 2 * x + 1 - place.c
        for j in range(CHUNKS):
            link.arrived(piece(other, j), ss.at[0, 0], rs.at[other, j])
    keep.wait()


def gather_zy(place, link, block, plane, other_plane, sems):
    zs, zr, ys, yr, ss, sr = sems
    half = place.nz // 2
    gy = lambda z, d: z * NY + (place.y + d + NY) % NY
    for k in range(half + 3):
        for q, z, way in slots(place, k):
            here = block(gy(z, 0))
            if k > 0:
                link.arrived(here, zs.at[q], zr.at[q])
            if k == 0:
                link.send(here, here, zs.at[1], zr.at[1], place.zn(1))
                if half > 1:
                    link.send(here, here, zs.at[half + 1], zr.at[half + 1], place.zn(-1))
            elif way == 1 and k < half:
                link.send(here, here, zs.at[q + 1], zr.at[q + 1], place.zn(1))
            elif way == -1 and k < half - 1:
                link.send(here, here, zs.at[q + 1], zr.at[q + 1], place.zn(-1))
            link.send(here, here, ys.at[0, q], yr.at[0, q], place.yn(1))
            link.send(here, here, ys.at[1, q], yr.at[1, q], place.yn(-1))
        for q, z, way in slots(place, k - 1) if k >= 1 else []:
            near = block(gy(z, -way))
            kind = 0 if way == 1 else 1
            link.arrived(near, zs.at[0], yr.at[kind, q])
            link.send(near, near, ys.at[2, q], yr.at[2, q], place.yn(way))
        for q, z, way in slots(place, k - 2) if k >= 2 else []:
            link.arrived(block(gy(z, way)), zs.at[0], yr.at[1 if way == 1 else 0, q])
            link.arrived(block(gy(z, 2)), zs.at[0], yr.at[2, q])
            link.send(plane(z), plane(z), ss.at[q], sr.at[q], place.sib)
        yield
    for k in range(half + 1):
        for q, z, way in slots(place, k):
            link.arrived(other_plane(z), zs.at[0], sr.at[q])


def gather_yz(place, link, block, plane, other_plane, sems):
    zs, zr, ys, yr, ss, sr = sems
    half = place.nz // 2
    gy = lambda d: place.z * NY + (place.y + d + NY) % NY
    here = block(gy(0))
    link.send(here, here, ys.at[0], yr.at[0], place.yn(1))
    link.send(here, here, ys.at[1], yr.at[1], place.yn(-1))
    yield
    near = block(gy(-1))
    link.arrived(near, zs.at[0], yr.at[0])
    link.send(near, near, ys.at[2], yr.at[2], place.yn(1))
    link.arrived(block(gy(1)), zs.at[0], yr.at[1])
    link.arrived(block(gy(2)), zs.at[0], yr.at[2])
    for k in range(half + 1):
        for q, z, way in slots(place, k):
            here = plane(z)
            if k > 0:
                link.arrived(here, zs.at[q], zr.at[q])
            if k == 0:
                link.send(here, here, zs.at[1], zr.at[1], place.zn(1))
                if half > 1:
                    link.send(here, here, zs.at[half + 1], zr.at[half + 1], place.zn(-1))
            elif way == 1 and k < half:
                link.send(here, here, zs.at[q + 1], zr.at[q + 1], place.zn(1))
            elif way == -1 and k < half - 1:
                link.send(here, here, zs.at[q + 1], zr.at[q + 1], place.zn(-1))
            link.send(here, here, ss.at[q], sr.at[q], place.sib)
        yield
    for k in range(half + 1):
        for q, z, way in slots(place, k):
            link.arrived(other_plane(z), zs.at[0], sr.at[q])


def gather_out(place, link, wo_all, xs, xr, first, second):
    g, c = place.g, place.c
    own = wo_all.at[place.x, c, g]
    for n, d in enumerate((1, -1, 2)):
        link.send(own, own, xs.at[n], xr.at[n], place.xn(d))
    yield
    for n, d in enumerate((1, -1, 2)):
        link.arrived(wo_all.at[(place.x - d + NX) % NX, c, g], xs.at[0], xr.at[n])
    half = NX // 2
    low = lambda g: wo_all.at[pl.ds(0, half), c, g]
    high = lambda g: wo_all.at[pl.ds(half, half), c, g]
    low_plane = lambda c: lambda z: wo_all.at[pl.ds(0, half), c, pl.ds(z * NY, NY)]
    high_plane = lambda c: lambda z: wo_all.at[pl.ds(half, half), c, pl.ds(z * NY, NY)]
    gens = [
        gather_zy(place, link, low, low_plane(c), low_plane(1 - c), first),
        gather_yz(place, link, high, high_plane(c), high_plane(1 - c), second),
    ]
    yield from together(gens)


def together(gens):
    gens = list(gens)
    while gens:
        for gen in list(gens):
            if next(gen, "end") == "end":
                gens.remove(gen)
        yield


def gather_kernel(nz, tok, w, wo, tok_all, w_all, wo_all, ls, ts, tr, *sems):
    place = Place(nz)
    link = Link(place)
    g, c = place.g, place.c
    width = w.shape[1] // 2
    lanes = lambda start, size: pl.ds(pl.multiple_of(start, 128), size)
    keep = [
        pltpu.make_async_copy(w, w_all.at[g, :, lanes(c * width, 2 * width)], ls.at[0]),
        pltpu.make_async_copy(wo, wo_all.at[place.x, c, g], ls.at[1]),
    ]
    for copy in keep:
        copy.start()
    barrier(
        [place.zn(1), place.zn(-1), place.yn(1), place.yn(-1)]
        + [place.xn(1), place.xn(-1), place.xn(2), place.sib]
    )
    for copy in keep:
        copy.wait()
    block = lambda g: w_all.at[g, :, lanes(c * width, 2 * width)]
    plane = lambda z: w_all.at[pl.ds(z * NY, NY), :, lanes(c * 2 * width, width)]
    other = lambda z: w_all.at[pl.ds(z * NY, NY), :, lanes((1 - c) * 2 * width, width)]
    gens = [
        gather_zy(place, link, block, plane, other, sems[0:6]),
        gather_rows(place, link, tok, tok_all, ts, tr),
        gather_out(place, link, wo_all, sems[6], sems[7], sems[8:14], sems[14:20]),
    ]
    for _ in together(gens):
        pass
    link.finish()


def gather_call(nz, tok, w, wo):
    rows, model = tok.shape
    depth, width = w.shape[0], w.shape[1] // 2
    grp = nz * NY
    ring = [DMA((nz,)), DMA((nz,)), DMA((3, nz)), DMA((3, nz)), DMA((nz,)), DMA((nz,))]
    plain = [DMA((nz,)), DMA((nz,)), DMA((3,)), DMA((3,)), DMA((nz,)), DMA((nz,))]
    return pl.pallas_call(
        functools.partial(gather_kernel, nz),
        out_shape=(
            jax.ShapeDtypeStruct((NS, rows, model), BF16),
            jax.ShapeDtypeStruct((grp, depth, 3 * width), BF16),
            jax.ShapeDtypeStruct((NX, 2, grp) + wo.shape, BF16),
        ),
        in_specs=[ANY] * 3,
        out_specs=[ANY] * 3,
        scratch_shapes=[DMA((2,)), DMA((8, CHUNKS)), DMA((NS, CHUNKS))]
        + ring
        + [DMA((3,)), DMA((3,))]
        + ring
        + plain,
        compiler_params=pltpu.CompilerParams(collective_id=0, has_side_effects=True),
        name="gather",
    )(tok, w, wo)


def exchange_kernel(nz, att, kv, att_in, kv_in, ls, ss, rs):
    place = Place(nz)
    link = Link(place)
    s = place.s
    keep = pltpu.make_async_copy(att.at[s], att_in.at[s], ls)
    keep.start()
    barrier([place.sn(d) for d in range(1, NS)])
    for d in range(1, NS):
        to = (s + d) % NS
        link.send(att.at[to], att_in.at[s], ss.at[d], rs.at[d], {"seq": to})
    link.send(kv, kv_in, ss.at[0], rs.at[0], place.xn(2))
    for d in range(1, NS):
        link.arrived(att_in.at[(s - d + NS) % NS], ss.at[0], rs.at[d])
    link.arrived(kv_in, ss.at[0], rs.at[0])
    keep.wait()
    link.finish()


def exchange_call(nz, att, kv):
    return pl.pallas_call(
        functools.partial(exchange_kernel, nz),
        out_shape=(
            jax.ShapeDtypeStruct(att.shape, BF16),
            jax.ShapeDtypeStruct(kv.shape, BF16),
        ),
        in_specs=[ANY] * 2,
        out_specs=[ANY] * 2,
        scratch_shapes=[DMA, DMA((NS,)), DMA((NS,))],
        compiler_params=pltpu.CompilerParams(collective_id=1, has_side_effects=True),
        name="exchange",
    )(att, kv)


def head_kernel(
    nz, st, gain, embed, norm_out, max_out,
    emb, own, zbuf, rows, buf, m1, m2, m3,
    ls, s1, r1, s2, r2, s3, r3, s4, r4, s5, r5, s6, r6, s7, r7,
):
    place = Place(nz)
    link = Link(place)
    s, y, z, c = place.s, place.y, place.z, place.c
    fetch = pltpu.make_async_copy(embed, emb, ls)
    fetch.start()
    seq_peers = [place.sn(d) for d in range(1, NS)]
    y_peers = [place.yn(d) for d in range(1, NY)]
    z_peers = [place.zn(d) for d in range(1, nz)]
    barrier(seq_peers + y_peers + z_peers)
    own[s] = st[s]
    for d in range(1, NS):
        to = (s + d) % NS
        link.send(st.at[to], own.at[s], s1.at[d], r1.at[d], {"seq": to})
    for d in range(1, NS):
        link.arrived(own.at[(s - d + NS) % NS], s1.at[0], r1.at[d])
    zbuf[z] = jnp.sum(own[...], axis=0)
    for d in range(1, nz):
        link.send(zbuf.at[z], zbuf.at[z], s2.at[d], r2.at[d], place.zn(d))
    for d in range(1, nz):
        link.arrived(zbuf.at[(z - d + nz) % nz], s2.at[0], r2.at[d])
    for n in range(nz):
        rows[n * SEGS : (n + 1) * SEGS] = zbuf[n]
    buf[s, y] = rows[...].astype(BF16)
    for d in range(1, NY):
        link.send(buf.at[s, y], buf.at[s, y], s3.at[d], r3.at[d], place.yn(d))
    for d in range(1, NY):
        link.arrived(buf.at[s, (y - d + NY) % NY], s3.at[0], r3.at[d])
    link.send(buf.at[s], buf.at[s], s4.at[0], r4.at[0], place.sib)
    for d in range(1, NX):
        link.send(buf.at[s], buf.at[s], s4.at[d], r4.at[d], place.xn(d))
    for d in (1, 3, 2):
        came = buf.at[place.xs(-d)]
        link.arrived(came, s4.at[0], r4.at[d])
        link.send(came, came, s5.at[d], r5.at[d], place.sib)
    for d in range(NX):
        came = buf.at[2 * ((place.x - d + NX) % NX) + 1 - c]
        link.arrived(came, s4.at[0], r4.at[0] if d == 0 else r5.at[d])
    count = NY * nz * SEGS
    width = buf.shape[-1]
    total = jnp.zeros((count, 1), F32)
    for n in range(NS):
        value = buf[n].reshape(count, width).astype(F32)
        total = total + jnp.sum(value * value, axis=1, keepdims=True)
    mean = total / (NS * width)
    norm_out[...] = jnp.sqrt(mean)
    scale = lax.rsqrt(mean + eps)
    fetch.wait()
    logits = jnp.zeros((emb.shape[0], count), F32)
    for n in range(NS):
        value = buf[n].reshape(count, width).astype(F32)
        final = (value * scale * gain[:, n * width : (n + 1) * width]).astype(BF16)
        logits = logits + lax.dot_general(
            emb[:, n * width : (n + 1) * width],
            final,
            (((1,), (1,)), ((), ())),
            preferred_element_type=F32,
        )
    m1[s] = jnp.max(logits, axis=0, keepdims=True)
    for d in range(1, NS):
        link.send(m1.at[s], m1.at[s], s6.at[d], r6.at[d], place.sn(d))
    for d in range(1, NS):
        link.arrived(m1.at[(s - d + NS) % NS], s6.at[0], r6.at[d])
    m2[y] = jnp.max(m1[...], axis=0)
    for d in range(1, NY):
        link.send(m2.at[y], m2.at[y], s7.at[d], r7.at[d], place.yn(d))
    for d in range(1, NY):
        link.arrived(m2.at[(y - d + NY) % NY], s7.at[0], r7.at[d])
    m3[z] = jnp.max(m2[...], axis=0)
    for d in range(1, nz):
        link.send(m3.at[z], m3.at[z], s7.at[NY + d], r7.at[NY + d], place.zn(d))
    for d in range(1, nz):
        link.arrived(m3.at[(z - d + nz) % nz], s7.at[0], r7.at[NY + d])
    max_out[...] = cap_value * jnp.tanh(jnp.max(m3[...], axis=0) / cap_value)
    link.finish()


def head_call(nz, st, gain, embed):
    count = NY * nz * SEGS
    width = st.shape[-1]
    return pl.pallas_call(
        functools.partial(head_kernel, nz),
        out_shape=(
            jax.ShapeDtypeStruct((count, 1), F32),
            jax.ShapeDtypeStruct((1, count), F32),
        ),
        in_specs=[VMEM, VMEM, ANY],
        out_specs=[VMEM, VMEM],
        scratch_shapes=[
            pltpu.VMEM(embed.shape, BF16),
            pltpu.VMEM((NS, SEGS, width), F32),
            pltpu.VMEM((nz, SEGS, width), F32),
            pltpu.VMEM((nz * SEGS, width), F32),
            pltpu.VMEM((NS, NY, nz * SEGS, width), BF16),
            pltpu.VMEM((NS, 1, count), F32),
            pltpu.VMEM((NY, 1, count), F32),
            pltpu.VMEM((nz, 1, count), F32),
            DMA,
            DMA((NS,)), DMA((NS,)),
            DMA((nz,)), DMA((nz,)),
            DMA((NY,)), DMA((NY,)),
            DMA((NX,)), DMA((NX,)),
            DMA((NX,)), DMA((NX,)),
            DMA((NS,)), DMA((NS,)),
            DMA((NY + nz,)), DMA((NY + nz,)),
        ],
        compiler_params=pltpu.CompilerParams(
            collective_id=2, has_side_effects=True, vmem_limit_bytes=32 * 1024 * 1024
        ),
        name="head",
    )(st, gain, embed)


def rows_scaled(value_rows, scales):
    mean_square = jnp.mean(value_rows * value_rows, axis=-1, keepdims=True)
    return value_rows * lax.rsqrt(mean_square + eps) * scales


def rotate(value_rows, offsets):
    half_width = value_rows.shape[-1] // 2
    frequency = rope_base ** (
        -2.0 * jnp.arange(half_width, dtype=F32) / value_rows.shape[-1]
    )
    angles = offsets.astype(F32)[:, None] * frequency[None, :]
    cosine, sine = jnp.cos(angles), jnp.sin(angles)
    lower, upper = value_rows[:, :half_width], value_rows[:, half_width:]
    return jnp.concatenate(
        [lower * cosine - upper * sine, upper * cosine + lower * sine], axis=-1
    )


def shards(
    tokens, seg_ids, deal, page_table, in_gain, w_query, key_weight, value_weight,
    q_gain, key_gain, w_out, post_gain, final_gain, embed,
):
    nz = lax.axis_size("grp") // NY
    own_tokens = tokens[0]
    rows, model = own_tokens.shape
    segment, pos = seg_ids[0], deal[0]
    pack = pos.shape[0]
    width = q_gain.shape[0]
    s = lax.axis_index("seq")
    own_start = s * rows

    normed = rows_scaled(own_tokens.astype(F32), in_gain).astype(BF16)
    group = s // (NS // KEY_HEADS) * width
    w_key = lax.dynamic_slice_in_dim(key_weight, group, width, 1)
    w_value = lax.dynamic_slice_in_dim(value_weight, group, width, 1)
    even = s % 2 == 0
    w_own = jnp.concatenate(
        [jnp.where(even, w_key, w_query), jnp.where(even, w_query, w_value)], axis=1
    )
    tok_all, w_all, wo_all = gather_call(nz, normed, w_own, w_out.T)

    ends = jnp.sum(
        (segment[None, :] <= jnp.arange(SEGS, dtype=jnp.int32)[:, None]).astype(jnp.int32), axis=1
    )
    start = jnp.max(jnp.where(pos[:, None] >= ends[None, :], ends[None, :], 0), axis=1)
    offsets = pos - start

    raw = jnp.dot(
        tok_all.reshape(pack, model), w_all.reshape(model, 3 * width), preferred_element_type=F32
    )
    key = rotate(rows_scaled(raw[:, :width], key_gain), offsets).astype(BF16)
    query = rotate(rows_scaled(raw[:, width : 2 * width], q_gain), offsets).astype(BF16)
    value = rows_scaled(raw[:, 2 * width :], 1.0).astype(BF16)

    scores = lax.dot_general(query, key, (((1,), (1,)), ((), ())), preferred_element_type=F32)
    allowed = (pos[None, :] <= pos[:, None]) & (pos[None, :] >= start[:, None])
    masked = jnp.where(allowed, scores, -1e30)
    peak = jnp.max(masked, axis=-1, keepdims=True)
    raw_weights = jnp.where(allowed, jnp.exp(masked - peak), 0.0)
    total = jnp.sum(raw_weights, axis=-1, keepdims=True)
    weights = (raw_weights / total).astype(BF16)
    attended = jnp.dot(weights, value, preferred_element_type=F32).astype(BF16)

    pages = page_table[0]
    slots_page = pack // pages.shape[0]
    page_of = jnp.sum(
        jnp.where(
            (pos // slots_page)[:, None] == jnp.arange(pages.shape[0], dtype=jnp.int32)[None, :],
            pages[None, :],
            0,
        ),
        axis=1,
    )
    physical = page_of * slots_page + pos % slots_page
    both = jnp.concatenate([key, value], axis=1)
    partner = (s + NS // 2) % NS
    target = jnp.concatenate(
        [own_start + jnp.arange(rows, dtype=jnp.int32), partner * rows + jnp.arange(rows, dtype=jnp.int32)]
    )
    pick = (target[:, None] == physical[None, :]).astype(BF16)
    picked = jnp.dot(pick, both, preferred_element_type=F32).astype(BF16)

    att_in, kv_in = exchange_call(nz, attended.reshape(NS, rows, width), picked[rows:])
    first = s < NS // 2
    low = jnp.where(first, picked[:rows], kv_in)
    high = jnp.where(first, kv_in, picked[:rows])
    cache = jnp.concatenate(
        [low[:, :width], high[:, :width], low[:, width:], high[:, width:]], axis=1
    ).reshape(rows // slots_page, slots_page, 2 * KEY_HEADS * width)

    wo = wo_all.reshape(NS, model, width)
    summed = jnp.zeros((rows, model), F32)
    for n in range(NS):
        part = lax.dot_general(
            att_in[n], wo[n], (((1,), (1,)), ((), ())), preferred_element_type=F32
        )
        summed = summed + part.astype(BF16).astype(F32)
    hidden = (own_tokens.astype(F32) + rows_scaled(summed, post_gain)).astype(BF16)

    own_pos = lax.dynamic_slice_in_dim(pos, own_start, rows, 0)
    selector = (own_pos[None, :] == (ends - 1)[:, None]).astype(BF16)
    states = jnp.dot(selector, hidden, preferred_element_type=F32)
    states = states.reshape(SEGS, NS, width).transpose(1, 0, 2)
    norm, top = head_call(nz, states, final_gain[None, :], embed)
    order = lambda v: v.reshape(NY, nz, SEGS).transpose(1, 0, 2).reshape(-1)
    return (hidden[None], cache[None], order(norm), order(top))


def solution(mesh):
    return jax.shard_map(
        shards,
        mesh=mesh,
        in_specs=(
            P("grp", "seq", None),
            P("grp", None),
            P("grp", None),
            P("grp", None),
            P(),
            P("grp", "seq"),
            P("grp", None),
            P("grp", None),
            P(),
            P(),
            P("seq", "grp"),
            P(),
            P(),
            P(("grp", "seq"), None),
        ),
        out_specs=(P("grp", "seq", None), P("grp", "seq", None, None), P(), P()),
        check_vma=False,
    )
```

```python
import functools

import jax
import jax.numpy as jnp
from jax import lax
from jax.experimental import pallas as pl
from jax.experimental.pallas import tpu as pltpu
from jax.sharding import PartitionSpec as P

MESH = pl.DeviceIdType.MESH
ANY = pl.BlockSpec(memory_space=pl.ANY)
VMEM = pl.BlockSpec(memory_space=pltpu.VMEM)
BF16 = jnp.bfloat16
F32 = jnp.float32
DMA = pltpu.SemaphoreType.DMA

KEY_HEADS = 2
PAGE_SLOTS = 8
SEGS = 4
NY = 4
NX = 4
NS = 8
CHUNKS = 4
eps = 1e-06
rope_base = 1000000.0
cap_value = 30.0


def remote(src, dst, send_sem, recv_sem, device):
    return pltpu.make_async_remote_copy(
        src_ref=src,
        dst_ref=dst,
        send_sem=send_sem,
        recv_sem=recv_sem,
        device_id=device,
        device_id_type=MESH,
    )


class Place:
    def __init__(self, nz):
        self.nz = nz
        self.g = lax.axis_index("grp")
        self.s = lax.axis_index("seq")
        self.z, self.y = self.g // NY, self.g % NY
        self.x, self.c = self.s // 2, self.s % 2
        self.sib = {"seq": 2 * self.x + 1 - self.c}

    def zn(self, d):
        return {"grp": ((self.z + d + self.nz) % self.nz) * NY + self.y}

    def yn(self, d):
        return {"grp": self.z * NY + (self.y + d + NY) % NY}

    def xs(self, d):
        return 2 * ((self.x + d + NX) % NX) + self.c

    def xn(self, d):
        return {"seq": self.xs(d)}

    def sn(self, d):
        return {"seq": (self.s + d) % NS}


class Link:
    def __init__(self, place):
        self.place = place
        self.sent = []

    def send(self, src, dst, send_sem, recv_sem, device):
        copy = remote(src, dst, send_sem, recv_sem, device)
        copy.start()
        self.sent.append(copy)

    def arrived(self, dst, send_sem, recv_sem):
        remote(dst, dst, send_sem, recv_sem, self.place.sib).wait_recv()

    def finish(self):
        for copy in self.sent:
            copy.wait_send()


def slots(place, k):
    nz = place.nz
    half = nz // 2
    if k == 0:
        return [(0, place.z, 1)]
    if k > half:
        return []
    up = (k, (place.z - k + nz) % nz, 1)
    if k == half:
        return [up]
    return [up, (half + k, (place.z + k) % nz, -1)]


def gather_rows(place, link, every, ss, rs):
    step = every.shape[1] // CHUNKS
    piece = lambda s, j: every.at[s, pl.ds(j * step, step)]
    s, left, right, far = place.s, place.xs(-1), place.xs(1), place.xs(2)
    for j in range(CHUNKS):
        mine = piece(s, j)
        link.send(mine, mine, ss.at[0, j], rs.at[s, j], place.xn(1))
        link.send(mine, mine, ss.at[1, j], rs.at[s, j], place.xn(-1))
    for j in range(CHUNKS):
        link.send(piece(s, j), piece(s, j), ss.at[2, j], rs.at[s, j], place.sib)
    yield
    for j in range(CHUNKS):
        link.arrived(piece(left, j), ss.at[0, 0], rs.at[left, j])
        if 2 * j < CHUNKS:
            link.send(piece(left, j), piece(left, j), ss.at[3, j], rs.at[left, j], place.xn(1))
        link.send(piece(left, j), piece(left, j), ss.at[4, j], rs.at[left, j], place.sib)
        link.arrived(piece(right, j), ss.at[0, 0], rs.at[right, j])
        if 2 * j >= CHUNKS:
            link.send(piece(right, j), piece(right, j), ss.at[3, j], rs.at[right, j], place.xn(-1))
        link.send(piece(right, j), piece(right, j), ss.at[5, j], rs.at[right, j], place.sib)
        yield
    for j in range(CHUNKS):
        link.arrived(piece(far, j), ss.at[0, 0], rs.at[far, j])
        link.send(piece(far, j), piece(far, j), ss.at[6, j], rs.at[far, j], place.sib)
        yield
    for x in range(NX):
        other = 2 * x + 1 - place.c
        for j in range(CHUNKS):
            link.arrived(piece(other, j), ss.at[0, 0], rs.at[other, j])


def gather_zy(place, link, block, plane, other_plane, sems):
    zs, zr, ys, yr, ss, sr = sems
    half = place.nz // 2
    gy = lambda z, d: z * NY + (place.y + d + NY) % NY
    for k in range(half + 3):
        for q, z, way in slots(place, k):
            here = block(gy(z, 0))
            if k > 0:
                link.arrived(here, zs.at[q], zr.at[q])
            if k == 0:
                link.send(here, here, zs.at[1], zr.at[1], place.zn(1))
                if half > 1:
                    link.send(here, here, zs.at[half + 1], zr.at[half + 1], place.zn(-1))
            elif way == 1 and k < half:
                link.send(here, here, zs.at[q + 1], zr.at[q + 1], place.zn(1))
            elif way == -1 and k < half - 1:
                link.send(here, here, zs.at[q + 1], zr.at[q + 1], place.zn(-1))
            link.send(here, here, ys.at[0, q], yr.at[0, q], place.yn(1))
            link.send(here, here, ys.at[1, q], yr.at[1, q], place.yn(-1))
        for q, z, way in slots(place, k - 1) if k >= 1 else []:
            near = block(gy(z, -way))
            kind = 0 if way == 1 else 1
            link.arrived(near, zs.at[0], yr.at[kind, q])
            link.send(near, near, ys.at[2, q], yr.at[2, q], place.yn(way))
        for q, z, way in slots(place, k - 2) if k >= 2 else []:
            link.arrived(block(gy(z, way)), zs.at[0], yr.at[1 if way == 1 else 0, q])
            link.arrived(block(gy(z, 2)), zs.at[0], yr.at[2, q])
            link.send(plane(z), plane(z), ss.at[q], sr.at[q], place.sib)
        yield
    for k in range(half + 1):
        for q, z, way in slots(place, k):
            link.arrived(other_plane(z), zs.at[0], sr.at[q])


def gather_yz(place, link, block, plane, other_plane, sems):
    zs, zr, ys, yr, ss, sr = sems
    half = place.nz // 2
    gy = lambda d: place.z * NY + (place.y + d + NY) % NY
    here = block(gy(0))
    link.send(here, here, ys.at[0], yr.at[0], place.yn(1))
    link.send(here, here, ys.at[1], yr.at[1], place.yn(-1))
    yield
    near = block(gy(-1))
    link.arrived(near, zs.at[0], yr.at[0])
    link.send(near, near, ys.at[2], yr.at[2], place.yn(1))
    link.arrived(block(gy(1)), zs.at[0], yr.at[1])
    link.arrived(block(gy(2)), zs.at[0], yr.at[2])
    for k in range(half + 1):
        for q, z, way in slots(place, k):
            here = plane(z)
            if k > 0:
                link.arrived(here, zs.at[q], zr.at[q])
            if k == 0:
                link.send(here, here, zs.at[1], zr.at[1], place.zn(1))
                if half > 1:
                    link.send(here, here, zs.at[half + 1], zr.at[half + 1], place.zn(-1))
            elif way == 1 and k < half:
                link.send(here, here, zs.at[q + 1], zr.at[q + 1], place.zn(1))
            elif way == -1 and k < half - 1:
                link.send(here, here, zs.at[q + 1], zr.at[q + 1], place.zn(-1))
            link.send(here, here, ss.at[q], sr.at[q], place.sib)
        yield
    for k in range(half + 1):
        for q, z, way in slots(place, k):
            link.arrived(other_plane(z), zs.at[0], sr.at[q])


def together(gens):
    gens = list(gens)
    while gens:
        for gen in list(gens):
            if next(gen, "end") == "end":
                gens.remove(gen)
        yield


def pump(gen, steps):
    for _ in range(steps):
        next(gen, None)


def scaled(value, gain):
    mean_square = jnp.mean(value * value, axis=-1, keepdims=True)
    value = value * lax.rsqrt(mean_square + eps)
    return value if gain is None else value * gain


def rotated(value, cosine, sine):
    half = value.shape[-1] // 2
    lower, upper = value[:, :half], value[:, half:]
    return jnp.concatenate(
        [lower * cosine - upper * sine, upper * cosine + lower * sine], axis=-1
    )


def column(row):
    return jnp.broadcast_to(row, (128, 128)).T


def nt(a, b):
    return lax.dot_general(a, b, (((1,), (1,)), ((), ())), preferred_element_type=F32)


def whole_kernel(
    nz,
    tok, seg, pos, pages, in_gain, freq, wq, wk, wv, wo, q_gain, k_gain, post_gain, final_gain, embed,
    hidden_out, cache_out, norm_out, max_out,
    v, d,
):
    place = Place(nz)
    link = Link(place)
    g, s, x, y, z, c = place.g, place.s, place.x, place.y, place.z, place.c
    rows, model = tok.shape
    width = q_gain.shape[1]
    pack = pos.shape[1]
    lanes = lambda start, size: pl.ds(pl.multiple_of(start, 128), size)

    fetch = pltpu.make_async_copy(embed, v.emb, d.fetch)
    fetch.start()
    peers = (
        [place.sn(n) for n in range(1, NS)]
        + [place.yn(n) for n in range(1, NY)]
        + [place.zn(n) for n in range(1, nz)]
    )
    entry = pltpu.get_barrier_semaphore()
    for peer in peers:
        pl.semaphore_signal(entry, inc=1, device_id=peer, device_id_type=MESH)

    kv = jnp.where(c == 0, wk[:, lanes(x // 2 * width, width)], wv[:, lanes(x // 2 * width, width)])
    v.w_all[g, :, width : 2 * width] = wq[...]
    v.w_all[g, :, lanes(c * 2 * width, width)] = kv
    v.wo_all[x, c, g] = wo[...]
    v.tok_all[s] = scaled(tok[...].astype(F32), in_gain[...]).astype(BF16)
    segment = seg[...]
    position = pos[...].astype(F32)
    ends = [
        jnp.sum((segment <= j).astype(F32), axis=1, keepdims=True) for j in range(SEGS)
    ]
    start = jnp.zeros_like(position)
    for end in ends[:-1]:
        start = jnp.maximum(start, jnp.where(position >= end, end, 0.0))
    for n in range(pack // 128):
        block = slice(n * 128, (n + 1) * 128)
        pos_col, start_col = column(position[:, block]), column(start[:, block])
        v.pos_col[block], v.start_col[block] = pos_col, start_col
        angle = (pos_col - start_col) * freq[...]
        v.cos[block], v.sin[block] = jnp.cos(angle), jnp.sin(angle)

    pl.semaphore_wait(entry, len(peers))

    block = lambda g: v.w_all.at[g, :, lanes(c * width, 2 * width)]
    plane = lambda c: lambda z: v.w_all.at[pl.ds(z * NY, NY), :, lanes(c * 2 * width, width)]
    wo_block = lambda n: lambda g: v.wo_all.at[n, c, g]
    wo_plane = lambda n, c: lambda z: v.wo_all.at[n, c, pl.ds(z * NY, NY)]

    def flow(n, way):
        return way(place, link, wo_block(n), wo_plane(n, c), wo_plane(n, 1 - c), d.wo[n])

    first = together([
        gather_zy(place, link, block, plane(c), plane(1 - c), d.w),
        gather_rows(place, link, v.tok_all, d.ts, d.tr),
    ])
    next(first)
    own = v.wo_all.at[x, c, g]
    for n, way in enumerate((1, -1, 2)):
        link.send(own, own, d.xs.at[n], d.xr.at[n], place.xn(way))
    next(first)
    for n, way in enumerate((1, -1, 2)):
        link.arrived(v.wo_all.at[(x - way + NX) % NX, c, g], d.xs.at[0], d.xr.at[n])
    early = flow(0, gather_yz)
    for _ in first:
        pump(early, 1)
    late = together([flow(1, gather_yz), flow(2, gather_zy), flow(3, gather_zy)])
    background = together([early, late])

    pump(background, 1)
    rest = v.w_all[...].reshape(model, 3 * width)
    part = 4
    for n in range(NS // part):
        here = slice(n * part * rows, (n + 1) * part * rows)
        raw = jnp.dot(
            v.tok_all[n * part : (n + 1) * part].reshape(part * rows, model),
            rest,
            preferred_element_type=F32,
        )
        cosine, sine = v.cos[here], v.sin[here]
        key = rotated(scaled(raw[:, :width], k_gain[...]), cosine, sine)
        query = rotated(scaled(raw[:, width : 2 * width], q_gain[...]), cosine, sine)
        v.query[here] = query.astype(BF16)
        v.kv[here, :width] = key.astype(BF16)
        v.kv[here, width:] = scaled(raw[:, 2 * width :], None).astype(BF16)
        pump(background, 1)

    for n, way in enumerate((2, 1, -1, 0)):
        chip = (x + way + NX) % NX
        here = pl.ds(pl.multiple_of(chip * 2 * rows, 256), 2 * rows)
        scores = nt(v.query[here], v.kv[:, :width])
        allowed = (position <= v.pos_col[here, 0:1]) & (position >= v.start_col[here, 0:1])
        masked = jnp.where(allowed, scores, -1e30)
        raw = jnp.exp(masked - jnp.max(masked, axis=1, keepdims=True))
        weights = (raw / jnp.sum(raw, axis=1, keepdims=True)).astype(BF16)
        attended = jnp.dot(weights, v.kv[:, width:], preferred_element_type=F32).astype(BF16)
        v.att[2 * chip] = attended[:rows]
        v.att[2 * chip + 1] = attended[rows:]
        there = 2 * chip + 1 - c
        link.send(v.att.at[there], v.att_in.at[s], d.asend.at[n, 0], d.arecv.at[n, 0], {"seq": there})
        if way == 0:
            v.att_in[s] = v.att[s]
        else:
            there = 2 * chip + c
            link.send(
                v.att.at[there], v.att_in.at[s], d.asend.at[n, 1], d.arecv.at[n, 1], {"seq": there}
            )
        pump(background, 2)

    table = column(pages[...].astype(F32))
    whole, within = pos[...] // PAGE_SLOTS, pos[...] % PAGE_SLOTS
    count = pages.shape[1]
    match = lax.broadcasted_iota(jnp.int32, (count, pack), 0) == whole
    page = jnp.sum(jnp.where(match, table[:, 0:1], 0.0), axis=0, keepdims=True)
    physical = page.astype(jnp.int32) * PAGE_SLOTS + within
    slot = lax.broadcasted_iota(jnp.int32, (rows, pack), 0)
    partner = (s + NS // 2) % NS
    for n, owner in enumerate((partner, s)):
        pick = (slot + owner * rows == physical).astype(BF16)
        picked = jnp.dot(pick, v.kv[...], preferred_element_type=F32).astype(BF16)
        if n == 0:
            v.kv_out[...] = picked
            link.send(v.kv_out, v.kv_in, d.ks, d.kr, {"seq": partner})
            pump(background, 1)
        else:
            mine = x // 2 * width
            cache_out[:, lanes(mine, width)] = picked[:, :width]
            cache_out[:, lanes(KEY_HEADS * width + mine, width)] = picked[:, width:]
    for _ in background:
        pass
    for n, way in enumerate((2, 1, -1, 0)):
        chip = (x - way + NX) % NX
        link.arrived(v.att_in.at[2 * chip + 1 - c], d.asend.at[0, 0], d.arecv.at[n, 0])
        if way != 0:
            link.arrived(v.att_in.at[2 * chip + c], d.asend.at[0, 0], d.arecv.at[n, 1])

    span = 512
    depth = wo.shape[0]
    for m in range(model // span):
        total = jnp.zeros((span, rows), F32)
        for n in range(NS):
            w = v.wo_all[n // 2, n % 2, m * span // depth : (m + 1) * span // depth]
            total = total + nt(w.reshape(span, width), v.att_in[n]).astype(BF16).astype(F32)
        for n in range(span // 128):
            v.summed[:, m * span + n * 128 : m * span + (n + 1) * 128] = total[
                n * 128 : (n + 1) * 128
            ].T
    hidden = (tok[...].astype(F32) + scaled(v.summed[...], post_gain[...])).astype(BF16)
    hidden_out[...] = hidden

    own_pos = pos[:, lanes(s * rows, rows)].astype(F32)
    line = lax.broadcasted_iota(jnp.int32, (16, rows), 0)
    last = jnp.full((16, rows), -1.0, F32)
    for j in range(SEGS):
        last = jnp.where(line == j, ends[j] - 1.0, last)
    select = (last == own_pos).astype(BF16)
    states = jnp.dot(select, hidden, preferred_element_type=F32)
    for n in range(NS):
        v.st[n] = states[:SEGS, n * width : (n + 1) * width]
    v.own[s] = v.st[s]
    for n in range(1, NS):
        to = (s + n) % NS
        link.send(v.st.at[to], v.own.at[s], d.s1.at[n], d.r1.at[n], {"seq": to})
    link.arrived(v.kv_in, d.ks, d.kr)
    other = (1 - x // 2) * width
    cache_out[:, lanes(other, width)] = v.kv_in[:, :width]
    cache_out[:, lanes(KEY_HEADS * width + other, width)] = v.kv_in[:, width:]
    for n in range(1, NS):
        link.arrived(v.own.at[(s - n + NS) % NS], d.s1.at[0], d.r1.at[n])
    v.zbuf[z] = jnp.sum(v.own[...], axis=0)
    for n in range(1, nz):
        link.send(v.zbuf.at[z], v.zbuf.at[z], d.s2.at[n], d.r2.at[n], place.zn(n))
    for n in range(1, nz):
        link.arrived(v.zbuf.at[(z - n + nz) % nz], d.s2.at[0], d.r2.at[n])
    for n in range(nz):
        v.rows[n * SEGS : (n + 1) * SEGS] = v.zbuf[n]
    v.buf[s, y] = v.rows[...].astype(BF16)
    for n in range(1, NY):
        link.send(v.buf.at[s, y], v.buf.at[s, y], d.s3.at[n], d.r3.at[n], place.yn(n))
    for n in range(1, NY):
        link.arrived(v.buf.at[s, (y - n + NY) % NY], d.s3.at[0], d.r3.at[n])
    for n in range(1, NX):
        link.send(v.buf.at[s], v.buf.at[s], d.s4.at[n], d.r4.at[n], place.xn(n))
    link.send(v.buf.at[s], v.buf.at[s], d.s4.at[0], d.r4.at[0], place.sib)
    for n in (1, 3, 2):
        came = v.buf.at[place.xs(-n)]
        link.arrived(came, d.s4.at[0], d.r4.at[n])
        link.send(came, came, d.s5.at[n], d.r5.at[n], place.sib)
    for n in range(NX):
        came = v.buf.at[2 * ((x - n + NX) % NX) + 1 - c]
        link.arrived(came, d.s4.at[0], d.r4.at[0] if n == 0 else d.r5.at[n])
    count = NY * nz * SEGS
    total = jnp.zeros((count, 1), F32)
    for n in range(NS):
        value = v.buf[n].reshape(count, width).astype(F32)
        total = total + jnp.sum(value * value, axis=1, keepdims=True)
    mean = total / model
    norm_out[...] = jnp.sqrt(mean)
    scale = lax.rsqrt(mean + eps)
    fetch.wait()
    logits = jnp.zeros((v.emb.shape[0], count), F32)
    for n in range(NS):
        value = v.buf[n].reshape(count, width).astype(F32)
        final = (value * scale * final_gain[:, n * width : (n + 1) * width]).astype(BF16)
        logits = logits + nt(v.emb[:, n * width : (n + 1) * width], final)
    v.m1[s] = jnp.max(logits, axis=0, keepdims=True)
    for n in range(1, NS):
        link.send(v.m1.at[s], v.m1.at[s], d.s6.at[n], d.r6.at[n], place.sn(n))
    for n in range(1, NS):
        link.arrived(v.m1.at[(s - n + NS) % NS], d.s6.at[0], d.r6.at[n])
    v.m2[y] = jnp.max(v.m1[...], axis=0)
    for n in range(1, NY):
        link.send(v.m2.at[y], v.m2.at[y], d.s7.at[n], d.r7.at[n], place.yn(n))
    for n in range(1, NY):
        link.arrived(v.m2.at[(y - n + NY) % NY], d.s7.at[0], d.r7.at[n])
    v.m3[z] = jnp.max(v.m2[...], axis=0)
    for n in range(1, nz):
        link.send(v.m3.at[z], v.m3.at[z], d.s8.at[n], d.r8.at[n], place.zn(n))
    for n in range(1, nz):
        link.arrived(v.m3.at[(z - n + nz) % nz], d.s8.at[0], d.r8.at[n])
    max_out[...] = cap_value * jnp.tanh(jnp.max(v.m3[...], axis=0) / cap_value)
    link.finish()


class Named:
    pass


def whole_call(nz, *args):
    tok, _, pos, _, _, freq, wq, wk, wv, wo, q_gain, _, _, _, embed = args
    rows, model = tok.shape
    pack, width = pos.shape[1], q_gain.shape[1]
    grp = nz * NY
    count = grp * SEGS
    ring = lambda: [DMA((nz,)), DMA((nz,)), DMA((3, nz)), DMA((3, nz)), DMA((nz,)), DMA((nz,))]
    plain = lambda: [DMA((nz,)), DMA((nz,)), DMA((3,)), DMA((3,)), DMA((nz,)), DMA((nz,))]
    buffers = dict(
        emb=(embed.shape, BF16),
        tok_all=((NS, rows, model), BF16),
        w_all=((grp, wq.shape[0], 3 * width), BF16),
        wo_all=((NX, 2, grp) + wo.shape, BF16),
        pos_col=((pack, 128), F32),
        start_col=((pack, 128), F32),
        cos=((pack, 128), F32),
        sin=((pack, 128), F32),
        query=((pack, width), BF16),
        kv=((pack, 2 * width), BF16),
        att=((NS, rows, width), BF16),
        att_in=((NS, rows, width), BF16),
        kv_out=((rows, 2 * width), BF16),
        kv_in=((rows, 2 * width), BF16),
        summed=((rows, model), F32),
        st=((NS, SEGS, width), F32),
        own=((NS, SEGS, width), F32),
        zbuf=((nz, SEGS, width), F32),
        rows=((nz * SEGS, width), F32),
        buf=((NS, NY, nz * SEGS, width), BF16),
        m1=((NS, 1, count), F32),
        m2=((NY, 1, count), F32),
        m3=((nz, 1, count), F32),
    )
    pair = lambda a, b, shape: {a: DMA(shape), b: DMA(shape)}
    sems = dict(fetch=DMA, ts=DMA((7, CHUNKS)), tr=DMA((NS, CHUNKS)), ks=DMA, kr=DMA)
    sems |= pair("xs", "xr", (3,)) | pair("asend", "arecv", (4, 2))
    sems |= pair("s1", "r1", (NS,)) | pair("s2", "r2", (nz,)) | pair("s3", "r3", (NY,))
    sems |= pair("s4", "r4", (NX,)) | pair("s5", "r5", (NX,)) | pair("s6", "r6", (NS,))
    sems |= pair("s7", "r7", (NY,)) | pair("s8", "r8", (nz,))
    flows = [ring(), plain(), plain(), ring(), ring()]
    scratch = (
        [pltpu.VMEM(*b) for b in buffers.values()]
        + list(sems.values())
        + [sem for one in flows for sem in one]
    )

    def kernel(*refs):
        refs, extra = list(refs[:19]), list(refs[19:])
        v, d = Named(), Named()
        for name in buffers:
            setattr(v, name, extra.pop(0))
        for name in sems:
            setattr(d, name, extra.pop(0))
        groups = [tuple(extra[6 * n : 6 * n + 6]) for n in range(len(flows))]
        d.w, d.wo = groups[0], groups[1:]
        whole_kernel(nz, *refs, v, d)

    return pl.pallas_call(
        kernel,
        out_shape=(
            jax.ShapeDtypeStruct((rows, model), BF16),
            jax.ShapeDtypeStruct((rows, 2 * KEY_HEADS * width), BF16),
            jax.ShapeDtypeStruct((count, 1), F32),
            jax.ShapeDtypeStruct((1, count), F32),
        ),
        in_specs=[VMEM] * 14 + [ANY],
        out_specs=[VMEM] * 4,
        scratch_shapes=scratch,
        compiler_params=pltpu.CompilerParams(
            collective_id=0, has_side_effects=True, vmem_limit_bytes=56 * 1024 * 1024
        ),
        name="whole",
    )(*args)


def shards(
    tokens, seg_ids, deal, page_table, in_gain, w_query, key_weight, value_weight,
    q_gain, key_gain, w_out, post_gain, final_gain, embed,
):
    nz = lax.axis_size("grp") // NY
    half = q_gain.shape[0] // 2
    frequency = rope_base ** (-2.0 * jnp.arange(half, dtype=F32) / q_gain.shape[0])
    hidden, cache, norm, top = whole_call(
        nz, tokens[0], seg_ids, deal, page_table, in_gain[None], frequency[None],
        w_query, key_weight, value_weight, w_out.T, q_gain[None], key_gain[None],
        post_gain[None], final_gain[None], embed,
    )
    pages = cache.shape[0] // PAGE_SLOTS
    cache = cache.reshape(pages, PAGE_SLOTS, cache.shape[1])
    order = lambda v: v.reshape(NY, nz, SEGS).transpose(1, 0, 2).reshape(-1)
    return (hidden[None], cache[None], order(norm), order(top))


def solution(mesh):
    return jax.shard_map(
        shards,
        mesh=mesh,
        in_specs=(
            P("grp", "seq", None),
            P("grp", None),
            P("grp", None),
            P("grp", None),
            P(),
            P("grp", "seq"),
            P("grp", None),
            P("grp", None),
            P(),
            P(),
            P("seq", "grp"),
            P(),
            P(),
            P(("grp", "seq"), None),
        ),
        out_specs=(P("grp", "seq", None), P("grp", "seq", None, None), P(), P()),
        check_vma=False,
    )
```

```python
import functools

import jax
import jax.numpy as jnp
from jax import lax
from jax.experimental import pallas as pl
from jax.experimental.pallas import tpu as pltpu
from jax.sharding import PartitionSpec as P

MESH = pl.DeviceIdType.MESH
ANY = pl.BlockSpec(memory_space=pl.ANY)
VMEM = pl.BlockSpec(memory_space=pltpu.VMEM)
BF16 = jnp.bfloat16
F32 = jnp.float32
DMA = pltpu.SemaphoreType.DMA

KEY_HEADS = 2
PAGE_SLOTS = 8
SEGS = 4
NY = 4
NX = 4
NS = 8
CHUNKS = 4
eps = 1e-06
rope_base = 1000000.0
cap_value = 30.0


def remote(src, dst, send_sem, recv_sem, device):
    return pltpu.make_async_remote_copy(
        src_ref=src,
        dst_ref=dst,
        send_sem=send_sem,
        recv_sem=recv_sem,
        device_id=device,
        device_id_type=MESH,
    )


class Place:
    def __init__(self, nz):
        self.nz = nz
        self.g = lax.axis_index("grp")
        self.s = lax.axis_index("seq")
        self.z, self.y = self.g // NY, self.g % NY
        self.x, self.c = self.s // 2, self.s % 2
        self.sib = {"seq": 2 * self.x + 1 - self.c}

    def zn(self, d):
        return {"grp": ((self.z + d + self.nz) % self.nz) * NY + self.y}

    def yn(self, d):
        return {"grp": self.z * NY + (self.y + d + NY) % NY}

    def xs(self, d):
        return 2 * ((self.x + d + NX) % NX) + self.c

    def xn(self, d):
        return {"seq": self.xs(d)}

    def sn(self, d):
        return {"seq": (self.s + d) % NS}


class Link:
    def __init__(self, place):
        self.place = place
        self.sent = []

    def send(self, src, dst, send_sem, recv_sem, device):
        copy = remote(src, dst, send_sem, recv_sem, device)
        copy.start()
        self.sent.append(copy)

    def arrived(self, dst, send_sem, recv_sem):
        remote(dst, dst, send_sem, recv_sem, self.place.sib).wait_recv()

    def finish(self):
        for copy in self.sent:
            copy.wait_send()


def slots(place, k):
    nz = place.nz
    half = nz // 2
    if k == 0:
        return [(0, place.z, 1)]
    if k > half:
        return []
    up = (k, (place.z - k + nz) % nz, 1)
    if k == half:
        return [up]
    return [up, (half + k, (place.z + k) % nz, -1)]


def gather_rows(place, link, every, ss, rs):
    step = every.shape[1] // CHUNKS
    piece = lambda s, j: every.at[s, pl.ds(j * step, step)]
    s, left, right, far = place.s, place.xs(-1), place.xs(1), place.xs(2)
    for j in range(CHUNKS):
        mine = piece(s, j)
        link.send(mine, mine, ss.at[0, j], rs.at[s, j], place.xn(1))
        link.send(mine, mine, ss.at[1, j], rs.at[s, j], place.xn(-1))
    for j in range(CHUNKS):
        link.send(piece(s, j), piece(s, j), ss.at[2, j], rs.at[s, j], place.sib)
    yield
    for j in range(CHUNKS):
        link.arrived(piece(left, j), ss.at[0, 0], rs.at[left, j])
        if 2 * j < CHUNKS:
            link.send(piece(left, j), piece(left, j), ss.at[3, j], rs.at[left, j], place.xn(1))
        link.send(piece(left, j), piece(left, j), ss.at[4, j], rs.at[left, j], place.sib)
        link.arrived(piece(right, j), ss.at[0, 0], rs.at[right, j])
        if 2 * j >= CHUNKS:
            link.send(piece(right, j), piece(right, j), ss.at[3, j], rs.at[right, j], place.xn(-1))
        link.send(piece(right, j), piece(right, j), ss.at[5, j], rs.at[right, j], place.sib)
        yield
    for j in range(CHUNKS):
        link.arrived(piece(far, j), ss.at[0, 0], rs.at[far, j])
        link.send(piece(far, j), piece(far, j), ss.at[6, j], rs.at[far, j], place.sib)
        yield
    for x in range(NX):
        other = 2 * x + 1 - place.c
        for j in range(CHUNKS):
            link.arrived(piece(other, j), ss.at[0, 0], rs.at[other, j])


def gather_zy(place, link, block, plane, other_plane, sems):
    zs, zr, ys, yr, ss, sr = sems
    half = place.nz // 2
    gy = lambda z, d: z * NY + (place.y + d + NY) % NY
    direct = [q for k in (half - 1, half) for q, _, _ in slots(place, k)]
    for k in range(half + 3):
        for q, z, way in slots(place, k):
            here = block(gy(z, 0))
            if k > 0:
                link.arrived(here, zs.at[q], zr.at[q])
            if k == 0:
                link.send(here, here, zs.at[1], zr.at[1], place.zn(1))
                if half > 1:
                    link.send(here, here, zs.at[half + 1], zr.at[half + 1], place.zn(-1))
            elif way == 1 and k < half:
                link.send(here, here, zs.at[q + 1], zr.at[q + 1], place.zn(1))
            elif way == -1 and k < half - 1:
                link.send(here, here, zs.at[q + 1], zr.at[q + 1], place.zn(-1))
            link.send(here, here, ys.at[0, q], yr.at[0, q], place.yn(1))
            link.send(here, here, ys.at[1, q], yr.at[1, q], place.yn(-1))
            if k >= half - 1:
                link.send(here, here, ys.at[2, q], yr.at[2, q], place.yn(2))
        for q, z, way in slots(place, k - 2) if 2 <= k <= half else []:
            near = block(gy(z, -way))
            kind = 0 if way == 1 else 1
            link.arrived(near, zs.at[0], yr.at[kind, q])
            link.send(near, near, ys.at[2, q], yr.at[2, q], place.yn(way))
        ready = [n for n in range(half + 1) if min(n + 4, half + 2) == k]
        for q, z, way in [slot for n in ready for slot in slots(place, n)]:
            link.arrived(block(gy(z, way)), zs.at[0], yr.at[1 if way == 1 else 0, q])
            if q in direct:
                link.arrived(block(gy(z, -way)), zs.at[0], yr.at[0 if way == 1 else 1, q])
            link.arrived(block(gy(z, 2)), zs.at[0], yr.at[2, q])
            link.send(plane(z), plane(z), ss.at[q], sr.at[q], place.sib)
        yield
    for k in range(half + 1):
        for q, z, way in slots(place, k):
            link.arrived(other_plane(z), zs.at[0], sr.at[q])


def gather_yz(place, link, block, plane, other_plane, sems):
    zs, zr, ys, yr, ss, sr = sems
    half = place.nz // 2
    gy = lambda d: place.z * NY + (place.y + d + NY) % NY
    here = block(gy(0))
    link.send(here, here, ys.at[0], yr.at[0], place.yn(1))
    link.send(here, here, ys.at[1], yr.at[1], place.yn(-1))
    yield
    near = block(gy(-1))
    link.arrived(near, zs.at[0], yr.at[0])
    link.send(near, near, ys.at[2], yr.at[2], place.yn(1))
    link.arrived(block(gy(1)), zs.at[0], yr.at[1])
    link.arrived(block(gy(2)), zs.at[0], yr.at[2])
    for k in range(half + 1):
        for q, z, way in slots(place, k):
            here = plane(z)
            if k > 0:
                link.arrived(here, zs.at[q], zr.at[q])
            if k == 0:
                link.send(here, here, zs.at[1], zr.at[1], place.zn(1))
                if half > 1:
                    link.send(here, here, zs.at[half + 1], zr.at[half + 1], place.zn(-1))
            elif way == 1 and k < half:
                link.send(here, here, zs.at[q + 1], zr.at[q + 1], place.zn(1))
            elif way == -1 and k < half - 1:
                link.send(here, here, zs.at[q + 1], zr.at[q + 1], place.zn(-1))
            link.send(here, here, ss.at[q], sr.at[q], place.sib)
        yield
    for k in range(half + 1):
        for q, z, way in slots(place, k):
            link.arrived(other_plane(z), zs.at[0], sr.at[q])


def together(gens):
    gens = list(gens)
    while gens:
        for gen in list(gens):
            if next(gen, "end") == "end":
                gens.remove(gen)
        yield


def pump(gen, steps):
    for _ in range(steps):
        next(gen, None)


def scaled(value, gain):
    mean_square = jnp.mean(value * value, axis=-1, keepdims=True)
    value = value * lax.rsqrt(mean_square + eps)
    return value if gain is None else value * gain


def rotated(value, cosine, sine):
    half = value.shape[-1] // 2
    lower, upper = value[:, :half], value[:, half:]
    return jnp.concatenate(
        [lower * cosine - upper * sine, upper * cosine + lower * sine], axis=-1
    )


def column(row):
    return jnp.broadcast_to(row, (128, 128)).T


def nt(a, b):
    return lax.dot_general(a, b, (((1,), (1,)), ((), ())), preferred_element_type=F32)


def whole_kernel(
    nz,
    tok, seg, pos, pages, in_gain, freq, wq, wk, wv, wo, q_gain, k_gain, post_gain, final_gain, embed,
    hidden_out, cache_out, norm_out, max_out,
    v, d,
):
    place = Place(nz)
    link = Link(place)
    g, s, x, y, z, c = place.g, place.s, place.x, place.y, place.z, place.c
    rows, model = tok.shape
    width = q_gain.shape[1]
    pack = pos.shape[1]
    lanes = lambda start, size: pl.ds(pl.multiple_of(start, 128), size)

    fetch = pltpu.make_async_copy(embed, v.emb, d.fetch)
    fetch.start()
    peers = (
        [place.sn(n) for n in range(1, NS)]
        + [place.yn(n) for n in range(1, NY)]
        + [place.zn(1), place.zn(-1)]
    )
    entry = pltpu.get_barrier_semaphore()
    for peer in peers:
        pl.semaphore_signal(entry, inc=1, device_id=peer, device_id_type=MESH)

    kv = jnp.where(c == 0, wk[:, lanes(x // 2 * width, width)], wv[:, lanes(x // 2 * width, width)])
    v.w_all[g, :, width : 2 * width] = wq[...]
    v.w_all[g, :, lanes(c * 2 * width, width)] = kv
    v.wo_all[x, c, g] = wo[...]
    v.tok_all[s] = scaled(tok[...].astype(F32), in_gain[...]).astype(BF16)
    segment = seg[...]
    position = pos[...].astype(F32)
    ends = [
        jnp.sum((segment <= j).astype(F32), axis=1, keepdims=True) for j in range(SEGS)
    ]
    start = jnp.zeros_like(position)
    for end in ends[:-1]:
        start = jnp.maximum(start, jnp.where(position >= end, end, 0.0))
    for n in range(pack // 128):
        block = slice(n * 128, (n + 1) * 128)
        pos_col, start_col = column(position[:, block]), column(start[:, block])
        v.pos_col[block], v.start_col[block] = pos_col, start_col
        angle = (pos_col - start_col) * freq[...]
        v.cos[block], v.sin[block] = jnp.cos(angle), jnp.sin(angle)

    pl.semaphore_wait(entry, len(peers))

    block = lambda g: v.w_all.at[g, :, lanes(c * width, 2 * width)]
    plane = lambda c: lambda z: v.w_all.at[pl.ds(z * NY, NY), :, lanes(c * 2 * width, width)]
    wo_block = lambda n: lambda g: v.wo_all.at[n, c, g]
    wo_plane = lambda n, c: lambda z: v.wo_all.at[n, c, pl.ds(z * NY, NY)]

    def flow(n, way):
        return way(place, link, wo_block(n), wo_plane(n, c), wo_plane(n, 1 - c), d.wo[n])

    weights = gather_zy(place, link, block, plane(c), plane(1 - c), d.w)
    tokens = gather_rows(place, link, v.tok_all, d.ts, d.tr)
    background = together([
        flow(0, gather_yz), flow(1, gather_yz), flow(2, gather_zy), flow(3, gather_zy)
    ])
    own = v.wo_all.at[x, c, g]
    for t in range(nz // 2 + 4):
        pump(weights, 1)
        if t in (0, 3, 4, 5, 6) or t >= 7:
            pump(tokens, 1)
        if t == 0:
            for n, way in enumerate((1, -1, 2)):
                link.send(own, own, d.xs.at[n], d.xr.at[n], place.xn(way))
        if t == 1:
            for n, way in enumerate((1, -1, 2)):
                link.arrived(v.wo_all.at[(x - way + NX) % NX, c, g], d.xs.at[0], d.xr.at[n])
        if t >= 2:
            pump(background, 1)
    for _ in together([weights, tokens]):
        pass

    pump(background, 1)
    rest = v.w_all[...].reshape(model, 3 * width)
    part = 4
    for n in range(NS // part):
        here = slice(n * part * rows, (n + 1) * part * rows)
        raw = jnp.dot(
            v.tok_all[n * part : (n + 1) * part].reshape(part * rows, model),
            rest,
            preferred_element_type=F32,
        )
        cosine, sine = v.cos[here], v.sin[here]
        key = rotated(scaled(raw[:, :width], k_gain[...]), cosine, sine)
        query = rotated(scaled(raw[:, width : 2 * width], q_gain[...]), cosine, sine)
        v.query[here] = query.astype(BF16)
        v.kv[here, :width] = key.astype(BF16)
        v.kv[here, width:] = scaled(raw[:, 2 * width :], None).astype(BF16)
        pump(background, 1)

    for n, way in enumerate((2, 1, -1, 0)):
        chip = (x + way + NX) % NX
        here = pl.ds(pl.multiple_of(chip * 2 * rows, 256), 2 * rows)
        scores = nt(v.query[here], v.kv[:, :width])
        allowed = (position <= v.pos_col[here, 0:1]) & (position >= v.start_col[here, 0:1])
        masked = jnp.where(allowed, scores, -1e30)
        raw = jnp.exp(masked - jnp.max(masked, axis=1, keepdims=True))
        weights = (raw / jnp.sum(raw, axis=1, keepdims=True)).astype(BF16)
        attended = jnp.dot(weights, v.kv[:, width:], preferred_element_type=F32).astype(BF16)
        v.att[2 * chip] = attended[:rows]
        v.att[2 * chip + 1] = attended[rows:]
        there = 2 * chip + 1 - c
        link.send(v.att.at[there], v.att_in.at[s], d.asend.at[n, 0], d.arecv.at[n, 0], {"seq": there})
        if way == 0:
            v.att_in[s] = v.att[s]
        else:
            there = 2 * chip + c
            link.send(
                v.att.at[there], v.att_in.at[s], d.asend.at[n, 1], d.arecv.at[n, 1], {"seq": there}
            )
        pump(background, 1)

    table = column(pages[...].astype(F32))
    whole, within = pos[...] // PAGE_SLOTS, pos[...] % PAGE_SLOTS
    count = pages.shape[1]
    match = lax.broadcasted_iota(jnp.int32, (count, pack), 0) == whole
    page = jnp.sum(jnp.where(match, table[:, 0:1], 0.0), axis=0, keepdims=True)
    physical = page.astype(jnp.int32) * PAGE_SLOTS + within
    slot = lax.broadcasted_iota(jnp.int32, (rows, pack), 0)
    partner = (s + NS // 2) % NS
    for n, owner in enumerate((partner, s)):
        pick = (slot + owner * rows == physical).astype(BF16)
        picked = jnp.dot(pick, v.kv[...], preferred_element_type=F32).astype(BF16)
        if n == 0:
            v.kv_out[...] = picked
            link.send(v.kv_out, v.kv_in, d.ks, d.kr, {"seq": partner})
            pump(background, 1)
        else:
            mine = x // 2 * width
            cache_out[:, lanes(mine, width)] = picked[:, :width]
            cache_out[:, lanes(KEY_HEADS * width + mine, width)] = picked[:, width:]
    for _ in background:
        pass
    for n, way in enumerate((2, 1, -1, 0)):
        chip = (x - way + NX) % NX
        link.arrived(v.att_in.at[2 * chip + 1 - c], d.asend.at[0, 0], d.arecv.at[n, 0])
        if way != 0:
            link.arrived(v.att_in.at[2 * chip + c], d.asend.at[0, 0], d.arecv.at[n, 1])

    span = 512
    depth = wo.shape[0]
    for m in range(model // span):
        total = jnp.zeros((span, rows), F32)
        for n in range(NS):
            w = v.wo_all[n // 2, n % 2, m * span // depth : (m + 1) * span // depth]
            total = total + nt(w.reshape(span, width), v.att_in[n]).astype(BF16).astype(F32)
        for n in range(span // 128):
            v.summed[:, m * span + n * 128 : m * span + (n + 1) * 128] = total[
                n * 128 : (n + 1) * 128
            ].T
    hidden = (tok[...].astype(F32) + scaled(v.summed[...], post_gain[...])).astype(BF16)
    hidden_out[...] = hidden

    own_pos = pos[:, lanes(s * rows, rows)].astype(F32)
    line = lax.broadcasted_iota(jnp.int32, (16, rows), 0)
    last = jnp.full((16, rows), -1.0, F32)
    for j in range(SEGS):
        last = jnp.where(line == j, ends[j] - 1.0, last)
    select = (last == own_pos).astype(BF16)
    states = jnp.dot(select, hidden, preferred_element_type=F32)
    for n in range(NS):
        v.st[n] = states[:SEGS, n * width : (n + 1) * width]
    v.own[s] = v.st[s]
    for n in range(1, NS):
        to = (s + n) % NS
        link.send(v.st.at[to], v.own.at[s], d.s1.at[n], d.r1.at[n], {"seq": to})
    link.arrived(v.kv_in, d.ks, d.kr)
    other = (1 - x // 2) * width
    cache_out[:, lanes(other, width)] = v.kv_in[:, :width]
    cache_out[:, lanes(KEY_HEADS * width + other, width)] = v.kv_in[:, width:]
    for n in range(1, NS):
        link.arrived(v.own.at[(s - n + NS) % NS], d.s1.at[0], d.r1.at[n])
    v.zbuf[z] = jnp.sum(v.own[...], axis=0)
    for n in range(1, nz):
        link.send(v.zbuf.at[z], v.zbuf.at[z], d.s2.at[n], d.r2.at[n], place.zn(n))
    for n in range(1, nz):
        link.arrived(v.zbuf.at[(z - n + nz) % nz], d.s2.at[0], d.r2.at[n])
    for n in range(nz):
        v.rows[n * SEGS : (n + 1) * SEGS] = v.zbuf[n]
    v.buf[s, y] = v.rows[...].astype(BF16)
    for n in range(1, NY):
        link.send(v.buf.at[s, y], v.buf.at[s, y], d.s3.at[n], d.r3.at[n], place.yn(n))
    for n in range(1, NY):
        link.arrived(v.buf.at[s, (y - n + NY) % NY], d.s3.at[0], d.r3.at[n])
    for n in range(1, NX):
        link.send(v.buf.at[s], v.buf.at[s], d.s4.at[n], d.r4.at[n], place.xn(n))
    link.send(v.buf.at[s], v.buf.at[s], d.s4.at[0], d.r4.at[0], place.sib)
    for n in (1, 3, 2):
        came = v.buf.at[place.xs(-n)]
        link.arrived(came, d.s4.at[0], d.r4.at[n])
        link.send(came, came, d.s5.at[n], d.r5.at[n], place.sib)
    for n in range(NX):
        came = v.buf.at[2 * ((x - n + NX) % NX) + 1 - c]
        link.arrived(came, d.s4.at[0], d.r4.at[0] if n == 0 else d.r5.at[n])
    count = NY * nz * SEGS
    total = jnp.zeros((count, 1), F32)
    for n in range(NS):
        value = v.buf[n].reshape(count, width).astype(F32)
        total = total + jnp.sum(value * value, axis=1, keepdims=True)
    mean = total / model
    norm_row = jnp.broadcast_to(jnp.sqrt(mean), (count, 128)).T[:8]
    scale = lax.rsqrt(mean + eps)
    fetch.wait()
    logits = jnp.zeros((v.emb.shape[0], count), F32)
    for n in range(NS):
        value = v.buf[n].reshape(count, width).astype(F32)
        final = (value * scale * final_gain[:, n * width : (n + 1) * width]).astype(BF16)
        logits = logits + nt(v.emb[:, n * width : (n + 1) * width], final)
    v.m1[s] = jnp.max(logits, axis=0, keepdims=True)
    for n in range(1, NS):
        link.send(v.m1.at[s], v.m1.at[s], d.s6.at[n], d.r6.at[n], place.sn(n))
    for n in range(1, NS):
        link.arrived(v.m1.at[(s - n + NS) % NS], d.s6.at[0], d.r6.at[n])
    v.m2[y] = jnp.max(v.m1[...], axis=0)
    for n in range(1, NY):
        link.send(v.m2.at[y], v.m2.at[y], d.s7.at[n], d.r7.at[n], place.yn(n))
    for n in range(1, NY):
        link.arrived(v.m2.at[(y - n + NY) % NY], d.s7.at[0], d.r7.at[n])
    v.m3[z] = jnp.max(v.m2[...], axis=0)
    for n in range(1, nz):
        link.send(v.m3.at[z], v.m3.at[z], d.s8.at[n], d.r8.at[n], place.zn(n))
    for n in range(1, nz):
        link.arrived(v.m3.at[(z - n + nz) % nz], d.s8.at[0], d.r8.at[n])
    top = cap_value * jnp.tanh(jnp.max(v.m3[...], axis=0) / cap_value)
    both = jnp.where(lax.broadcasted_iota(jnp.int32, (8, count), 0) == 0, top, norm_row)
    line = lax.broadcasted_iota(jnp.int32, (count, count), 0)
    place_of = lax.broadcasted_iota(jnp.int32, (count, count), 1)
    line_of = (
        place_of // SEGS % NY * (nz * SEGS) + place_of // (NY * SEGS) * SEGS + place_of % SEGS
    )
    both = jnp.dot(
        both,
        (line == line_of).astype(F32),
        precision=lax.Precision.HIGHEST,
        preferred_element_type=F32,
    )
    max_out[...] = both[0:1]
    norm_out[...] = both[1:2]
    link.finish()


class Named:
    pass


def whole_call(nz, *args):
    tok, _, pos, _, _, freq, wq, wk, wv, wo, q_gain, _, _, _, embed = args
    rows, model = tok.shape
    pack, width = pos.shape[1], q_gain.shape[1]
    grp = nz * NY
    count = grp * SEGS
    ring = lambda: [DMA((nz,)), DMA((nz,)), DMA((3, nz)), DMA((3, nz)), DMA((nz,)), DMA((nz,))]
    plain = lambda: [DMA((nz,)), DMA((nz,)), DMA((3,)), DMA((3,)), DMA((nz,)), DMA((nz,))]
    buffers = dict(
        emb=(embed.shape, BF16),
        tok_all=((NS, rows, model), BF16),
        w_all=((grp, wq.shape[0], 3 * width), BF16),
        wo_all=((NX, 2, grp) + wo.shape, BF16),
        pos_col=((pack, 128), F32),
        start_col=((pack, 128), F32),
        cos=((pack, 128), F32),
        sin=((pack, 128), F32),
        query=((pack, width), BF16),
        kv=((pack, 2 * width), BF16),
        att=((NS, rows, width), BF16),
        att_in=((NS, rows, width), BF16),
        kv_out=((rows, 2 * width), BF16),
        kv_in=((rows, 2 * width), BF16),
        summed=((rows, model), F32),
        st=((NS, SEGS, width), F32),
        own=((NS, SEGS, width), F32),
        zbuf=((nz, SEGS, width), F32),
        rows=((nz * SEGS, width), F32),
        buf=((NS, NY, nz * SEGS, width), BF16),
        m1=((NS, 1, count), F32),
        m2=((NY, 1, count), F32),
        m3=((nz, 1, count), F32),
    )
    pair = lambda a, b, shape: {a: DMA(shape), b: DMA(shape)}
    sems = dict(fetch=DMA, ts=DMA((7, CHUNKS)), tr=DMA((NS, CHUNKS)), ks=DMA, kr=DMA)
    sems |= pair("xs", "xr", (3,)) | pair("asend", "arecv", (4, 2))
    sems |= pair("s1", "r1", (NS,)) | pair("s2", "r2", (nz,)) | pair("s3", "r3", (NY,))
    sems |= pair("s4", "r4", (NX,)) | pair("s5", "r5", (NX,)) | pair("s6", "r6", (NS,))
    sems |= pair("s7", "r7", (NY,)) | pair("s8", "r8", (nz,))
    flows = [ring(), plain(), plain(), ring(), ring()]
    scratch = (
        [pltpu.VMEM(*b) for b in buffers.values()]
        + list(sems.values())
        + [sem for one in flows for sem in one]
    )

    def kernel(*refs):
        refs, extra = list(refs[:19]), list(refs[19:])
        v, d = Named(), Named()
        for name in buffers:
            setattr(v, name, extra.pop(0))
        for name in sems:
            setattr(d, name, extra.pop(0))
        groups = [tuple(extra[6 * n : 6 * n + 6]) for n in range(len(flows))]
        d.w, d.wo = groups[0], groups[1:]
        whole_kernel(nz, *refs, v, d)

    return pl.pallas_call(
        kernel,
        out_shape=(
            jax.ShapeDtypeStruct((rows, model), BF16),
            jax.ShapeDtypeStruct((rows, 2 * KEY_HEADS * width), BF16),
            jax.ShapeDtypeStruct((1, count), F32),
            jax.ShapeDtypeStruct((1, count), F32),
        ),
        in_specs=[VMEM] * 14 + [ANY],
        out_specs=[VMEM] * 4,
        scratch_shapes=scratch,
        compiler_params=pltpu.CompilerParams(
            collective_id=0, has_side_effects=True, vmem_limit_bytes=56 * 1024 * 1024
        ),
        name="whole",
    )(*args)


def store_kernel(*refs):
    half = len(refs) // 2
    for source, target in zip(refs[:half], refs[half:]):
        target[...] = source[...]


def store_call(*arrays):
    return pl.pallas_call(
        store_kernel,
        out_shape=[jax.ShapeDtypeStruct(a.shape, a.dtype) for a in arrays],
        in_specs=[VMEM] * len(arrays),
        out_specs=[VMEM] * len(arrays),
        name="store",
    )(*arrays)


def shards(
    tokens, seg_ids, deal, page_table, in_gain, w_query, key_weight, value_weight,
    q_gain, key_gain, w_out, post_gain, final_gain, embed,
):
    nz = lax.axis_size("grp") // NY
    half = q_gain.shape[0] // 2
    frequency = rope_base ** (-2.0 * jnp.arange(half, dtype=F32) / q_gain.shape[0])
    hidden, cache, norm, top = whole_call(
        nz, tokens[0], seg_ids, deal, page_table, in_gain[None], frequency[None],
        w_query, key_weight, value_weight, w_out.T, q_gain[None], key_gain[None],
        post_gain[None], final_gain[None], embed,
    )
    hidden, cache, norm, top = store_call(hidden, cache, norm, top)
    pages = cache.shape[0] // PAGE_SLOTS
    cache = cache.reshape(pages, PAGE_SLOTS, cache.shape[1])
    return (hidden[None], cache[None], norm[0], top[0])


def solution(mesh):
    return jax.shard_map(
        shards,
        mesh=mesh,
        in_specs=(
            P("grp", "seq", None),
            P("grp", None),
            P("grp", None),
            P("grp", None),
            P(),
            P("grp", "seq"),
            P("grp", None),
            P("grp", None),
            P(),
            P(),
            P("seq", "grp"),
            P(),
            P(),
            P(("grp", "seq"), None),
        ),
        out_specs=(P("grp", "seq", None), P("grp", "seq", None, None), P(), P()),
        check_vma=False,
    )
```

```python
import functools

import jax
import jax.numpy as jnp
from jax import lax
from jax.experimental import pallas as pl
from jax.experimental.pallas import tpu as pltpu
from jax.sharding import PartitionSpec as P

MESH = pl.DeviceIdType.MESH
ANY = pl.BlockSpec(memory_space=pl.ANY)
VMEM = pl.BlockSpec(memory_space=pltpu.VMEM)
BF16 = jnp.bfloat16
F32 = jnp.float32
DMA = pltpu.SemaphoreType.DMA

KEY_HEADS = 2
PAGE_SLOTS = 8
SEGS = 4
NY = 4
NX = 4
NS = 8
CHUNKS = 4
eps = 1e-06
rope_base = 1000000.0
cap_value = 30.0


def remote(src, dst, send_sem, recv_sem, device):
    return pltpu.make_async_remote_copy(
        src_ref=src,
        dst_ref=dst,
        send_sem=send_sem,
        recv_sem=recv_sem,
        device_id=device,
        device_id_type=MESH,
    )


class Place:
    def __init__(self, nz):
        self.nz = nz
        self.g = lax.axis_index("grp")
        self.s = lax.axis_index("seq")
        self.z, self.y = self.g // NY, self.g % NY
        self.x, self.c = self.s // 2, self.s % 2
        self.sib = {"seq": 2 * self.x + 1 - self.c}

    def zn(self, d):
        return {"grp": ((self.z + d + self.nz) % self.nz) * NY + self.y}

    def yn(self, d):
        return {"grp": self.z * NY + (self.y + d + NY) % NY}

    def xs(self, d):
        return 2 * ((self.x + d + NX) % NX) + self.c

    def xn(self, d):
        return {"seq": self.xs(d)}

    def sn(self, d):
        return {"seq": (self.s + d) % NS}


class Link:
    def __init__(self, place):
        self.place = place
        self.sent = []

    def send(self, src, dst, send_sem, recv_sem, device):
        copy = remote(src, dst, send_sem, recv_sem, device)
        copy.start()
        self.sent.append(copy)

    def arrived(self, dst, send_sem, recv_sem):
        remote(dst, dst, send_sem, recv_sem, self.place.sib).wait_recv()

    def finish(self):
        for copy in self.sent:
            copy.wait_send()


def slots(place, k):
    nz = place.nz
    half = nz // 2
    if k == 0:
        return [(0, place.z, 1)]
    if k > half:
        return []
    up = (k, (place.z - k + nz) % nz, 1)
    if k == half:
        return [up]
    return [up, (half + k, (place.z + k) % nz, -1)]


def gather_rows(place, link, every, ss, rs):
    step = every.shape[1] // CHUNKS
    piece = lambda s, j: every.at[s, pl.ds(j * step, step)]
    s, left, right, far = place.s, place.xs(-1), place.xs(1), place.xs(2)
    for j in range(CHUNKS):
        mine = piece(s, j)
        link.send(mine, mine, ss.at[0, j], rs.at[s, j], place.xn(1))
        link.send(mine, mine, ss.at[1, j], rs.at[s, j], place.xn(-1))
    for j in range(CHUNKS):
        link.send(piece(s, j), piece(s, j), ss.at[2, j], rs.at[s, j], place.sib)
    yield
    for j in range(CHUNKS):
        link.arrived(piece(left, j), ss.at[0, 0], rs.at[left, j])
        if 2 * j < CHUNKS:
            link.send(piece(left, j), piece(left, j), ss.at[3, j], rs.at[left, j], place.xn(1))
        link.send(piece(left, j), piece(left, j), ss.at[4, j], rs.at[left, j], place.sib)
        link.arrived(piece(right, j), ss.at[0, 0], rs.at[right, j])
        if 2 * j >= CHUNKS:
            link.send(piece(right, j), piece(right, j), ss.at[3, j], rs.at[right, j], place.xn(-1))
        link.send(piece(right, j), piece(right, j), ss.at[5, j], rs.at[right, j], place.sib)
        yield
    for j in range(CHUNKS):
        link.arrived(piece(far, j), ss.at[0, 0], rs.at[far, j])
        link.send(piece(far, j), piece(far, j), ss.at[6, j], rs.at[far, j], place.sib)
        yield
    for x in range(NX):
        other = 2 * x + 1 - place.c
        for j in range(CHUNKS):
            link.arrived(piece(other, j), ss.at[0, 0], rs.at[other, j])


def gather_zy(place, link, block, plane, other_plane, sems):
    zs, zr, ys, yr, ss, sr = sems
    half = place.nz // 2
    gy = lambda z, d: z * NY + (place.y + d + NY) % NY
    direct = [q for k in (half - 1, half) for q, _, _ in slots(place, k)]
    for k in range(half + 3):
        for q, z, way in slots(place, k):
            here = block(gy(z, 0))
            if k > 0:
                link.arrived(here, zs.at[q], zr.at[q])
            if k == 0:
                link.send(here, here, zs.at[1], zr.at[1], place.zn(1))
                if half > 1:
                    link.send(here, here, zs.at[half + 1], zr.at[half + 1], place.zn(-1))
            elif way == 1 and k < half:
                link.send(here, here, zs.at[q + 1], zr.at[q + 1], place.zn(1))
            elif way == -1 and k < half - 1:
                link.send(here, here, zs.at[q + 1], zr.at[q + 1], place.zn(-1))
            link.send(here, here, ys.at[0, q], yr.at[0, q], place.yn(1))
            link.send(here, here, ys.at[1, q], yr.at[1, q], place.yn(-1))
            if k >= half - 1:
                link.send(here, here, ys.at[2, q], yr.at[2, q], place.yn(2))
        for q, z, way in slots(place, k - 2) if 2 <= k <= half else []:
            near = block(gy(z, -way))
            kind = 0 if way == 1 else 1
            link.arrived(near, zs.at[0], yr.at[kind, q])
            link.send(near, near, ys.at[2, q], yr.at[2, q], place.yn(way))
        ready = [n for n in range(half + 1) if min(n + 4, half + 2) == k]
        for q, z, way in [slot for n in ready for slot in slots(place, n)]:
            link.arrived(block(gy(z, way)), zs.at[0], yr.at[1 if way == 1 else 0, q])
            if q in direct:
                link.arrived(block(gy(z, -way)), zs.at[0], yr.at[0 if way == 1 else 1, q])
            link.arrived(block(gy(z, 2)), zs.at[0], yr.at[2, q])
            link.send(plane(z), plane(z), ss.at[q], sr.at[q], place.sib)
        yield
    for k in range(half + 1):
        for q, z, way in slots(place, k):
            link.arrived(other_plane(z), zs.at[0], sr.at[q])


def gather_yz(place, link, block, plane, other_plane, sems):
    zs, zr, ys, yr, ss, sr = sems
    half = place.nz // 2
    gy = lambda d: place.z * NY + (place.y + d + NY) % NY
    here = block(gy(0))
    link.send(here, here, ys.at[0], yr.at[0], place.yn(1))
    link.send(here, here, ys.at[1], yr.at[1], place.yn(-1))
    yield
    near = block(gy(-1))
    link.arrived(near, zs.at[0], yr.at[0])
    link.send(near, near, ys.at[2], yr.at[2], place.yn(1))
    link.arrived(block(gy(1)), zs.at[0], yr.at[1])
    link.arrived(block(gy(2)), zs.at[0], yr.at[2])
    for k in range(half + 1):
        for q, z, way in slots(place, k):
            here = plane(z)
            if k > 0:
                link.arrived(here, zs.at[q], zr.at[q])
            if k == 0:
                link.send(here, here, zs.at[1], zr.at[1], place.zn(1))
                if half > 1:
                    link.send(here, here, zs.at[half + 1], zr.at[half + 1], place.zn(-1))
            elif way == 1 and k < half:
                link.send(here, here, zs.at[q + 1], zr.at[q + 1], place.zn(1))
            elif way == -1 and k < half - 1:
                link.send(here, here, zs.at[q + 1], zr.at[q + 1], place.zn(-1))
            link.send(here, here, ss.at[q], sr.at[q], place.sib)
        yield
    for k in range(half + 1):
        for q, z, way in slots(place, k):
            link.arrived(other_plane(z), zs.at[0], sr.at[q])


def together(gens):
    gens = list(gens)
    while gens:
        for gen in list(gens):
            if next(gen, "end") == "end":
                gens.remove(gen)
        yield


def pump(gen, steps):
    for _ in range(steps):
        next(gen, None)


def scaled(value, gain):
    mean_square = jnp.mean(value * value, axis=-1, keepdims=True)
    value = value * lax.rsqrt(mean_square + eps)
    return value if gain is None else value * gain


def rotated(value, cosine, sine):
    half = value.shape[-1] // 2
    lower, upper = value[:, :half], value[:, half:]
    return jnp.concatenate(
        [lower * cosine - upper * sine, upper * cosine + lower * sine], axis=-1
    )


def column(row):
    return jnp.broadcast_to(row, (128, 128)).T


def nt(a, b):
    return lax.dot_general(a, b, (((1,), (1,)), ((), ())), preferred_element_type=F32)


def whole_kernel(
    nz,
    tok, seg, pos, pages, in_gain, freq, wq, wk, wv, wo, q_gain, k_gain, post_gain, final_gain, embed,
    hidden_out, cache_out, norm_out, max_out,
    v, d,
):
    place = Place(nz)
    link = Link(place)
    g, s, x, y, z, c = place.g, place.s, place.x, place.y, place.z, place.c
    rows, model = tok.shape
    width = q_gain.shape[1]
    pack = pos.shape[1]
    lanes = lambda start, size: pl.ds(pl.multiple_of(start, 128), size)

    fetch = pltpu.make_async_copy(embed, v.emb, d.fetch)
    fetch.start()
    peers = (
        [place.sn(n) for n in range(1, NS)]
        + [place.yn(n) for n in range(1, NY)]
        + [place.zn(1), place.zn(-1)]
    )
    entry = pltpu.get_barrier_semaphore()
    for peer in peers:
        pl.semaphore_signal(entry, inc=1, device_id=peer, device_id_type=MESH)

    kv = jnp.where(c == 0, wk[:, lanes(x // 2 * width, width)], wv[:, lanes(x // 2 * width, width)])
    v.w_all[g, :, width : 2 * width] = wq[...]
    v.w_all[g, :, lanes(c * 2 * width, width)] = kv
    v.wo_all[x, c, g] = wo[...]
    v.tok_all[s] = scaled(tok[...].astype(F32), in_gain[...]).astype(BF16)
    segment = seg[...]
    position = pos[...].astype(F32)
    ends = [
        jnp.sum((segment <= j).astype(F32), axis=1, keepdims=True) for j in range(SEGS)
    ]
    start = jnp.zeros_like(position)
    for end in ends[:-1]:
        start = jnp.maximum(start, jnp.where(position >= end, end, 0.0))
    v.la[...] = jnp.zeros_like(v.la)

    def bounds(size):
        line = lax.broadcasted_iota(jnp.int32, (16, size), 0)
        first, last = jnp.zeros((16, size), F32), jnp.full((16, size), -1.0, F32)
        for j in range(SEGS):
            last = jnp.where(line == j, ends[j] - 1.0, last)
            if j > 0:
                first = jnp.where(line == j, ends[j - 1], first)
        return first, last

    def rope_tables():
        for n in range(pack // 128):
            block = slice(n * 128, (n + 1) * 128)
            pos_col, start_col = column(position[:, block]), column(start[:, block])
            v.pos_col[block], v.start_col[block] = pos_col, start_col
            angle = (pos_col - start_col) * freq[...]
            v.cos[block], v.sin[block] = jnp.cos(angle), jnp.sin(angle)
            yield

    pl.semaphore_wait(entry, len(peers))

    block = lambda g: v.w_all.at[g, :, lanes(c * width, 2 * width)]
    plane = lambda c: lambda z: v.w_all.at[pl.ds(z * NY, NY), :, lanes(c * 2 * width, width)]
    wo_block = lambda n: lambda g: v.wo_all.at[n, c, g]
    wo_plane = lambda n, c: lambda z: v.wo_all.at[n, c, pl.ds(z * NY, NY)]

    def flow(n, way):
        return way(place, link, wo_block(n), wo_plane(n, c), wo_plane(n, 1 - c), d.wo[n])

    weights = gather_zy(place, link, block, plane(c), plane(1 - c), d.w)
    tokens = gather_rows(place, link, v.tok_all, d.ts, d.tr)
    background = together([
        flow(0, gather_yz), flow(1, gather_yz), flow(2, gather_zy), flow(3, gather_zy)
    ])
    tables = rope_tables()
    own = v.wo_all.at[x, c, g]
    for t in range(nz // 2 + 4):
        pump(weights, 1)
        if t in (0, 3, 4, 5, 6) or t >= 7:
            pump(tokens, 1)
        if t == 0:
            for n, way in enumerate((1, -1, 2)):
                link.send(own, own, d.xs.at[n], d.xr.at[n], place.xn(way))
            _, last = bounds(rows)
            select = (last == pos[:, lanes(s * rows, rows)].astype(F32)).astype(BF16)
            found = jnp.dot(select, tok[...], preferred_element_type=F32).astype(BF16)
            for n in range(NS):
                v.tl_out[n] = found[:, n * width : (n + 1) * width]
            v.tl_in[s] = v.tl_out[s]
            for n in range(1, NS):
                to = (s + n) % NS
                link.send(v.tl_out.at[to], v.tl_in.at[s], d.s1.at[n], d.r1.at[n], {"seq": to})
        if t == 1:
            for n, way in enumerate((1, -1, 2)):
                link.arrived(v.wo_all.at[(x - way + NX) % NX, c, g], d.xs.at[0], d.xr.at[n])
        if t >= 2:
            pump(background, 1)
        pump(tables, 1)
    for _ in together([weights, tokens, tables]):
        pass

    pump(background, 1)
    rest = v.w_all[...].reshape(model, 3 * width)
    part = 4
    for n in range(NS // part):
        here = slice(n * part * rows, (n + 1) * part * rows)
        raw = jnp.dot(
            v.tok_all[n * part : (n + 1) * part].reshape(part * rows, model),
            rest,
            preferred_element_type=F32,
        )
        cosine, sine = v.cos[here], v.sin[here]
        key = rotated(scaled(raw[:, :width], k_gain[...]), cosine, sine)
        query = rotated(scaled(raw[:, width : 2 * width], q_gain[...]), cosine, sine)
        v.query[here] = query.astype(BF16)
        v.kv[here, :width] = key.astype(BF16)
        v.kv[here, width:] = scaled(raw[:, 2 * width :], None).astype(BF16)
        pump(background, 1)

    first, last = bounds(pack)
    select = (last == position).astype(BF16)
    query = jnp.dot(select, v.query[...], preferred_element_type=F32).astype(BF16)
    masked = jnp.where(
        (position <= last) & (position >= first), nt(query, v.kv[:, :width]), -1e30
    )
    raw = jnp.exp(masked - jnp.max(masked, axis=1, keepdims=True))
    weights = (raw / jnp.sum(raw, axis=1, keepdims=True)).astype(BF16)
    attended = jnp.dot(weights, v.kv[:, width:], preferred_element_type=F32)
    v.la[s, 0:16] = attended.astype(BF16)
    mine = v.la.at[s, pl.ds(0, 16)]
    for n in range(1, NS):
        link.send(mine, mine, d.ls.at[n], d.lr.at[n], place.sn(n))
    for _ in background:
        pass
    for n in range(1, NS):
        link.arrived(v.la.at[(s - n + NS) % NS, pl.ds(0, 16)], d.ls.at[0], d.lr.at[n])
        link.arrived(v.tl_in.at[(s - n + NS) % NS], d.s1.at[0], d.r1.at[n])

    span = 512
    depth = wo.shape[0]

    def project(source):
        for m in range(model // span):
            total = jnp.zeros((span, rows), F32)
            for n in range(NS):
                w = v.wo_all[n // 2, n % 2, m * span // depth : (m + 1) * span // depth]
                total = total + nt(w.reshape(span, width), source[n]).astype(BF16).astype(F32)
            for n in range(span // 128):
                v.summed[:, m * span + n * 128 : m * span + (n + 1) * 128] = total[
                    n * 128 : (n + 1) * 128
                ].T

    project(v.la)
    total = v.summed[0:16]
    scale = lax.rsqrt(jnp.mean(total * total, axis=1, keepdims=True) + eps)
    here = lanes(s * width, width)
    total = v.summed[0:16, here] * scale * post_gain[:, here]
    states = (jnp.sum(v.tl_in[...].astype(F32), axis=0) + total).astype(BF16).astype(F32)
    v.zbuf[z] = states[:SEGS]
    for n in range(1, nz):
        link.send(v.zbuf.at[z], v.zbuf.at[z], d.s2.at[n], d.r2.at[n], place.zn(n))

    for n, way in enumerate((2, 1, -1, 0)):
        chip = (x + way + NX) % NX
        here = pl.ds(pl.multiple_of(chip * 2 * rows, 256), 2 * rows)
        scores = nt(v.query[here], v.kv[:, :width])
        allowed = (position <= v.pos_col[here, 0:1]) & (position >= v.start_col[here, 0:1])
        masked = jnp.where(allowed, scores, -1e30)
        raw = jnp.exp(masked - jnp.max(masked, axis=1, keepdims=True))
        weights = (raw / jnp.sum(raw, axis=1, keepdims=True)).astype(BF16)
        attended = jnp.dot(weights, v.kv[:, width:], preferred_element_type=F32).astype(BF16)
        v.att[2 * chip] = attended[:rows]
        v.att[2 * chip + 1] = attended[rows:]
        there = 2 * chip + 1 - c
        link.send(v.att.at[there], v.att_in.at[s], d.asend.at[n, 0], d.arecv.at[n, 0], {"seq": there})
        if way == 0:
            v.att_in[s] = v.att[s]
        else:
            there = 2 * chip + c
            link.send(
                v.att.at[there], v.att_in.at[s], d.asend.at[n, 1], d.arecv.at[n, 1], {"seq": there}
            )

    for n in range(1, nz):
        link.arrived(v.zbuf.at[(z - n + nz) % nz], d.s2.at[0], d.r2.at[n])
    for n in range(nz):
        v.rows[n * SEGS : (n + 1) * SEGS] = v.zbuf[n]
    v.buf[s, y] = v.rows[...].astype(BF16)
    for n in range(1, NY):
        link.send(v.buf.at[s, y], v.buf.at[s, y], d.s3.at[n], d.r3.at[n], place.yn(n))

    table = column(pages[...].astype(F32))
    whole, within = pos[...] // PAGE_SLOTS, pos[...] % PAGE_SLOTS
    count = pages.shape[1]
    match = lax.broadcasted_iota(jnp.int32, (count, pack), 0) == whole
    page = jnp.sum(jnp.where(match, table[:, 0:1], 0.0), axis=0, keepdims=True)
    physical = page.astype(jnp.int32) * PAGE_SLOTS + within
    slot = lax.broadcasted_iota(jnp.int32, (rows, pack), 0)
    partner = (s + NS // 2) % NS
    for n, owner in enumerate((partner, s)):
        pick = (slot + owner * rows == physical).astype(BF16)
        picked = jnp.dot(pick, v.kv[...], preferred_element_type=F32).astype(BF16)
        if n == 0:
            v.kv_out[...] = picked
            link.send(v.kv_out, v.kv_in, d.ks, d.kr, {"seq": partner})
        else:
            mine = x // 2 * width
            cache_out[:, lanes(mine, width)] = picked[:, :width]
            cache_out[:, lanes(KEY_HEADS * width + mine, width)] = picked[:, width:]

    for n in range(1, NY):
        link.arrived(v.buf.at[s, (y - n + NY) % NY], d.s3.at[0], d.r3.at[n])
    for n in range(1, NX):
        link.send(v.buf.at[s], v.buf.at[s], d.s4.at[n], d.r4.at[n], place.xn(n))
    link.send(v.buf.at[s], v.buf.at[s], d.s4.at[0], d.r4.at[0], place.sib)

    for n, way in enumerate((2, 1, -1, 0)):
        chip = (x - way + NX) % NX
        link.arrived(v.att_in.at[2 * chip + 1 - c], d.asend.at[0, 0], d.arecv.at[n, 0])
        if way != 0:
            link.arrived(v.att_in.at[2 * chip + c], d.asend.at[0, 0], d.arecv.at[n, 1])
    project(v.att_in)
    hidden = tok[...].astype(F32) + scaled(v.summed[...], post_gain[...])
    hidden_out[...] = hidden.astype(BF16)
    link.arrived(v.kv_in, d.ks, d.kr)
    other = (1 - x // 2) * width
    cache_out[:, lanes(other, width)] = v.kv_in[:, :width]
    cache_out[:, lanes(KEY_HEADS * width + other, width)] = v.kv_in[:, width:]

    for n in (1, 3, 2):
        came = v.buf.at[place.xs(-n)]
        link.arrived(came, d.s4.at[0], d.r4.at[n])
        link.send(came, came, d.s5.at[n], d.r5.at[n], place.sib)
    for n in range(NX):
        came = v.buf.at[2 * ((x - n + NX) % NX) + 1 - c]
        link.arrived(came, d.s4.at[0], d.r4.at[0] if n == 0 else d.r5.at[n])
    count = NY * nz * SEGS
    total = jnp.zeros((count, 1), F32)
    for n in range(NS):
        value = v.buf[n].reshape(count, width).astype(F32)
        total = total + jnp.sum(value * value, axis=1, keepdims=True)
    mean = total / model
    norm_row = jnp.broadcast_to(jnp.sqrt(mean), (count, 128)).T[:8]
    scale = lax.rsqrt(mean + eps)
    fetch.wait()
    logits = jnp.zeros((v.emb.shape[0], count), F32)
    for n in range(NS):
        value = v.buf[n].reshape(count, width).astype(F32)
        final = (value * scale * final_gain[:, n * width : (n + 1) * width]).astype(BF16)
        logits = logits + nt(v.emb[:, n * width : (n + 1) * width], final)
    near = [(a, b) for a in range(NY) for b in range(NS)]
    v.m1[y * NS + s] = jnp.max(logits, axis=0, keepdims=True)
    for n, (a, b) in enumerate(near[1:], 1):
        to = {"grp": z * NY + (y + a) % NY, "seq": (s + b) % NS}
        link.send(v.m1.at[y * NS + s], v.m1.at[y * NS + s], d.s6.at[n], d.r6.at[n], to)
    for n, (a, b) in enumerate(near[1:], 1):
        slot = (y - a + NY) % NY * NS + (s - b + NS) % NS
        link.arrived(v.m1.at[slot], d.s6.at[0], d.r6.at[n])
    v.m3[z] = jnp.max(v.m1[...], axis=0)
    for n in range(1, nz):
        link.send(v.m3.at[z], v.m3.at[z], d.s8.at[n], d.r8.at[n], place.zn(n))
    for n in range(1, nz):
        link.arrived(v.m3.at[(z - n + nz) % nz], d.s8.at[0], d.r8.at[n])
    top = cap_value * jnp.tanh(jnp.max(v.m3[...], axis=0) / cap_value)
    both = jnp.where(lax.broadcasted_iota(jnp.int32, (8, count), 0) == 0, top, norm_row)
    line = lax.broadcasted_iota(jnp.int32, (count, count), 0)
    place_of = lax.broadcasted_iota(jnp.int32, (count, count), 1)
    line_of = (
        place_of // SEGS % NY * (nz * SEGS) + place_of // (NY * SEGS) * SEGS + place_of % SEGS
    )
    both = jnp.dot(
        both,
        (line == line_of).astype(F32),
        precision=lax.Precision.HIGHEST,
        preferred_element_type=F32,
    )
    max_out[...] = both[0:1]
    norm_out[...] = both[1:2]
    link.finish()


class Named:
    pass


def whole_call(nz, *args):
    tok, _, pos, _, _, freq, wq, wk, wv, wo, q_gain, _, _, _, embed = args
    rows, model = tok.shape
    pack, width = pos.shape[1], q_gain.shape[1]
    grp = nz * NY
    count = grp * SEGS
    ring = lambda: [DMA((nz,)), DMA((nz,)), DMA((3, nz)), DMA((3, nz)), DMA((nz,)), DMA((nz,))]
    plain = lambda: [DMA((nz,)), DMA((nz,)), DMA((3,)), DMA((3,)), DMA((nz,)), DMA((nz,))]
    buffers = dict(
        emb=(embed.shape, BF16),
        tok_all=((NS, rows, model), BF16),
        w_all=((grp, wq.shape[0], 3 * width), BF16),
        wo_all=((NX, 2, grp) + wo.shape, BF16),
        pos_col=((pack, 128), F32),
        start_col=((pack, 128), F32),
        cos=((pack, 128), F32),
        sin=((pack, 128), F32),
        query=((pack, width), BF16),
        kv=((pack, 2 * width), BF16),
        att=((NS, rows, width), BF16),
        att_in=((NS, rows, width), BF16),
        kv_out=((rows, 2 * width), BF16),
        kv_in=((rows, 2 * width), BF16),
        summed=((rows, model), F32),
        la=((NS, rows, width), BF16),
        tl_out=((NS, 16, width), BF16),
        tl_in=((NS, 16, width), BF16),
        zbuf=((nz, SEGS, width), F32),
        rows=((nz * SEGS, width), F32),
        buf=((NS, NY, nz * SEGS, width), BF16),
        m1=((NY * NS, 1, count), F32),
        m3=((nz, 1, count), F32),
    )
    pair = lambda a, b, shape: {a: DMA(shape), b: DMA(shape)}
    sems = dict(fetch=DMA, ts=DMA((7, CHUNKS)), tr=DMA((NS, CHUNKS)), ks=DMA, kr=DMA)
    sems |= pair("xs", "xr", (3,)) | pair("asend", "arecv", (4, 2))
    sems |= pair("s1", "r1", (NS,)) | pair("s2", "r2", (nz,)) | pair("s3", "r3", (NY,))
    sems |= pair("s4", "r4", (NX,)) | pair("s5", "r5", (NX,)) | pair("s6", "r6", (NY * NS,))
    sems |= pair("ls", "lr", (NS,)) | pair("s8", "r8", (nz,))
    flows = [ring(), plain(), plain(), ring(), ring()]
    scratch = (
        [pltpu.VMEM(*b) for b in buffers.values()]
        + list(sems.values())
        + [sem for one in flows for sem in one]
    )

    def kernel(*refs):
        refs, extra = list(refs[:19]), list(refs[19:])
        v, d = Named(), Named()
        for name in buffers:
            setattr(v, name, extra.pop(0))
        for name in sems:
            setattr(d, name, extra.pop(0))
        groups = [tuple(extra[6 * n : 6 * n + 6]) for n in range(len(flows))]
        d.w, d.wo = groups[0], groups[1:]
        whole_kernel(nz, *refs, v, d)

    return pl.pallas_call(
        kernel,
        out_shape=(
            jax.ShapeDtypeStruct((rows, model), BF16),
            jax.ShapeDtypeStruct((rows, 2 * KEY_HEADS * width), BF16),
            jax.ShapeDtypeStruct((1, count), F32),
            jax.ShapeDtypeStruct((1, count), F32),
        ),
        in_specs=[VMEM] * 14 + [ANY],
        out_specs=[VMEM] * 4,
        scratch_shapes=scratch,
        compiler_params=pltpu.CompilerParams(
            collective_id=0, has_side_effects=True, vmem_limit_bytes=56 * 1024 * 1024
        ),
        name="whole",
    )(*args)


def store_kernel(*refs):
    half = len(refs) // 2
    for source, target in zip(refs[:half], refs[half:]):
        target[...] = source[...]


def store_call(*arrays):
    return pl.pallas_call(
        store_kernel,
        out_shape=[jax.ShapeDtypeStruct(a.shape, a.dtype) for a in arrays],
        in_specs=[VMEM] * len(arrays),
        out_specs=[VMEM] * len(arrays),
        name="store",
    )(*arrays)


def shards(
    tokens, seg_ids, deal, page_table, in_gain, w_query, key_weight, value_weight,
    q_gain, key_gain, w_out, post_gain, final_gain, embed,
):
    nz = lax.axis_size("grp") // NY
    half = q_gain.shape[0] // 2
    frequency = rope_base ** (-2.0 * jnp.arange(half, dtype=F32) / q_gain.shape[0])
    hidden, cache, norm, top = whole_call(
        nz, tokens[0], seg_ids, deal, page_table, in_gain[None], frequency[None],
        w_query, key_weight, value_weight, w_out.T, q_gain[None], key_gain[None],
        post_gain[None], final_gain[None], embed,
    )
    hidden, cache, norm, top = store_call(hidden, cache, norm, top)
    pages = cache.shape[0] // PAGE_SLOTS
    cache = cache.reshape(pages, PAGE_SLOTS, cache.shape[1])
    return (hidden[None], cache[None], norm[0], top[0])


def solution(mesh):
    return jax.shard_map(
        shards,
        mesh=mesh,
        in_specs=(
            P("grp", "seq", None),
            P("grp", None),
            P("grp", None),
            P("grp", None),
            P(),
            P("grp", "seq"),
            P("grp", None),
            P("grp", None),
            P(),
            P(),
            P("seq", "grp"),
            P(),
            P(),
            P(("grp", "seq"), None),
        ),
        out_specs=(P("grp", "seq", None), P("grp", "seq", None, None), P(), P()),
        check_vma=False,
    )
```

```python
import functools

import jax
import jax.numpy as jnp
from jax import lax
from jax.experimental import pallas as pl
from jax.experimental.pallas import tpu as pltpu
from jax.sharding import PartitionSpec as P

MESH = pl.DeviceIdType.MESH
ANY = pl.BlockSpec(memory_space=pl.ANY)
VMEM = pl.BlockSpec(memory_space=pltpu.VMEM)
BF16 = jnp.bfloat16
F32 = jnp.float32
DMA = pltpu.SemaphoreType.DMA

KEY_HEADS = 2
PAGE_SLOTS = 8
SEGS = 4
NY = 4
NX = 4
NS = 8
CHUNKS = 4
eps = 1e-06
rope_base = 1000000.0
cap_value = 30.0


def remote(src, dst, send_sem, recv_sem, device):
    return pltpu.make_async_remote_copy(
        src_ref=src,
        dst_ref=dst,
        send_sem=send_sem,
        recv_sem=recv_sem,
        device_id=device,
        device_id_type=MESH,
    )


class Place:
    def __init__(self, nz):
        self.nz = nz
        self.g = lax.axis_index("grp")
        self.s = lax.axis_index("seq")
        self.z, self.y = self.g // NY, self.g % NY
        self.x, self.c = self.s // 2, self.s % 2
        self.sib = {"seq": 2 * self.x + 1 - self.c}

    def zn(self, d):
        return {"grp": ((self.z + d + self.nz) % self.nz) * NY + self.y}

    def yn(self, d):
        return {"grp": self.z * NY + (self.y + d + NY) % NY}

    def xs(self, d):
        return 2 * ((self.x + d + NX) % NX) + self.c

    def xn(self, d):
        return {"seq": self.xs(d)}

    def sn(self, d):
        return {"seq": (self.s + d) % NS}


class Link:
    def __init__(self, place):
        self.place = place
        self.sent = []

    def send(self, src, dst, send_sem, recv_sem, device):
        copy = remote(src, dst, send_sem, recv_sem, device)
        copy.start()
        self.sent.append(copy)

    def arrived(self, dst, send_sem, recv_sem):
        remote(dst, dst, send_sem, recv_sem, self.place.sib).wait_recv()

    def finish(self):
        for copy in self.sent:
            copy.wait_send()


def slots(place, k):
    nz = place.nz
    half = nz // 2
    if k == 0:
        return [(0, place.z, 1)]
    if k > half:
        return []
    up = (k, (place.z - k + nz) % nz, 1)
    if k == half:
        return [up]
    return [up, (half + k, (place.z + k) % nz, -1)]


def gather_rows(place, link, every, ss, rs):
    step = every.shape[1] // CHUNKS
    piece = lambda s, j: every.at[s, pl.ds(j * step, step)]
    s, left, right, far = place.s, place.xs(-1), place.xs(1), place.xs(2)
    for j in range(CHUNKS):
        mine = piece(s, j)
        link.send(mine, mine, ss.at[0, j], rs.at[s, j], place.xn(1))
        link.send(mine, mine, ss.at[1, j], rs.at[s, j], place.xn(-1))
    for j in range(CHUNKS):
        link.send(piece(s, j), piece(s, j), ss.at[2, j], rs.at[s, j], place.sib)
    yield
    for j in range(CHUNKS):
        link.arrived(piece(left, j), ss.at[0, 0], rs.at[left, j])
        if 2 * j < CHUNKS:
            link.send(piece(left, j), piece(left, j), ss.at[3, j], rs.at[left, j], place.xn(1))
        link.send(piece(left, j), piece(left, j), ss.at[4, j], rs.at[left, j], place.sib)
        link.arrived(piece(right, j), ss.at[0, 0], rs.at[right, j])
        if 2 * j >= CHUNKS:
            link.send(piece(right, j), piece(right, j), ss.at[3, j], rs.at[right, j], place.xn(-1))
        link.send(piece(right, j), piece(right, j), ss.at[5, j], rs.at[right, j], place.sib)
        yield
    for j in range(CHUNKS):
        link.arrived(piece(far, j), ss.at[0, 0], rs.at[far, j])
        link.send(piece(far, j), piece(far, j), ss.at[6, j], rs.at[far, j], place.sib)
        yield
    for x in range(NX):
        other = 2 * x + 1 - place.c
        for j in range(CHUNKS):
            link.arrived(piece(other, j), ss.at[0, 0], rs.at[other, j])


def gather_zy(place, link, block, plane, other_plane, sems):
    zs, zr, ys, yr, ss, sr = sems
    half = place.nz // 2
    gy = lambda z, d: z * NY + (place.y + d + NY) % NY
    direct = [q for k in (half - 1, half) for q, _, _ in slots(place, k)]
    for k in range(half + 3):
        for q, z, way in slots(place, k):
            here = block(gy(z, 0))
            if k > 0:
                link.arrived(here, zs.at[q], zr.at[q])
            if k == 0:
                link.send(here, here, zs.at[1], zr.at[1], place.zn(1))
                if half > 1:
                    link.send(here, here, zs.at[half + 1], zr.at[half + 1], place.zn(-1))
            elif way == 1 and k < half:
                link.send(here, here, zs.at[q + 1], zr.at[q + 1], place.zn(1))
            elif way == -1 and k < half - 1:
                link.send(here, here, zs.at[q + 1], zr.at[q + 1], place.zn(-1))
            link.send(here, here, ys.at[0, q], yr.at[0, q], place.yn(1))
            link.send(here, here, ys.at[1, q], yr.at[1, q], place.yn(-1))
            if k >= half - 1:
                link.send(here, here, ys.at[2, q], yr.at[2, q], place.yn(2))
        for q, z, way in slots(place, k - 2) if 2 <= k <= half else []:
            near = block(gy(z, -way))
            kind = 0 if way == 1 else 1
            link.arrived(near, zs.at[0], yr.at[kind, q])
            link.send(near, near, ys.at[2, q], yr.at[2, q], place.yn(way))
        ready = [n for n in range(half + 1) if min(n + 4, half + 2) == k]
        for q, z, way in [slot for n in ready for slot in slots(place, n)]:
            link.arrived(block(gy(z, way)), zs.at[0], yr.at[1 if way == 1 else 0, q])
            if q in direct:
                link.arrived(block(gy(z, -way)), zs.at[0], yr.at[0 if way == 1 else 1, q])
            link.arrived(block(gy(z, 2)), zs.at[0], yr.at[2, q])
            link.send(plane(z), plane(z), ss.at[q], sr.at[q], place.sib)
        yield
    for k in range(half + 1):
        for q, z, way in slots(place, k):
            link.arrived(other_plane(z), zs.at[0], sr.at[q])


def gather_yz(place, link, block, plane, other_plane, sems):
    zs, zr, ys, yr, ss, sr = sems
    half = place.nz // 2
    gy = lambda d: place.z * NY + (place.y + d + NY) % NY
    here = block(gy(0))
    link.send(here, here, ys.at[0], yr.at[0], place.yn(1))
    link.send(here, here, ys.at[1], yr.at[1], place.yn(-1))
    yield
    near = block(gy(-1))
    link.arrived(near, zs.at[0], yr.at[0])
    link.send(near, near, ys.at[2], yr.at[2], place.yn(1))
    link.arrived(block(gy(1)), zs.at[0], yr.at[1])
    link.arrived(block(gy(2)), zs.at[0], yr.at[2])
    for k in range(half + 1):
        for q, z, way in slots(place, k):
            here = plane(z)
            if k > 0:
                link.arrived(here, zs.at[q], zr.at[q])
            if k == 0:
                link.send(here, here, zs.at[1], zr.at[1], place.zn(1))
                if half > 1:
                    link.send(here, here, zs.at[half + 1], zr.at[half + 1], place.zn(-1))
            elif way == 1 and k < half:
                link.send(here, here, zs.at[q + 1], zr.at[q + 1], place.zn(1))
            elif way == -1 and k < half - 1:
                link.send(here, here, zs.at[q + 1], zr.at[q + 1], place.zn(-1))
            link.send(here, here, ss.at[q], sr.at[q], place.sib)
        yield
    for k in range(half + 1):
        for q, z, way in slots(place, k):
            link.arrived(other_plane(z), zs.at[0], sr.at[q])


def together(gens):
    gens = list(gens)
    while gens:
        for gen in list(gens):
            if next(gen, "end") == "end":
                gens.remove(gen)
        yield


def pump(gen, steps):
    for _ in range(steps):
        next(gen, None)


def scaled(value, gain):
    mean_square = jnp.mean(value * value, axis=-1, keepdims=True)
    value = value * lax.rsqrt(mean_square + eps)
    return value if gain is None else value * gain


def rotated(value, cosine, sine):
    half = value.shape[-1] // 2
    lower, upper = value[:, :half], value[:, half:]
    return jnp.concatenate(
        [lower * cosine - upper * sine, upper * cosine + lower * sine], axis=-1
    )


def column(row):
    return jnp.broadcast_to(row, (128, 128)).T


def nt(a, b):
    return lax.dot_general(a, b, (((1,), (1,)), ((), ())), preferred_element_type=F32)


def whole_kernel(
    nz,
    tok, seg, pos, pages, in_gain, freq, wq, wk, wv, wo, q_gain, k_gain, post_gain, final_gain, embed,
    hidden_out, cache_out, norm_out, max_out,
    v, d,
):
    place = Place(nz)
    link = Link(place)
    g, s, x, y, z, c = place.g, place.s, place.x, place.y, place.z, place.c
    rows, model = tok.shape
    width = q_gain.shape[1]
    pack = pos.shape[1]
    lanes = lambda start, size: pl.ds(pl.multiple_of(start, 128), size)

    fetch = pltpu.make_async_copy(embed, v.emb, d.fetch)
    fetch.start()
    peers = (
        [place.sn(n) for n in range(1, NS)]
        + [place.yn(n) for n in range(1, NY)]
        + [place.zn(1), place.zn(-1)]
    )
    entry = pltpu.get_barrier_semaphore()
    for peer in peers:
        pl.semaphore_signal(entry, inc=1, device_id=peer, device_id_type=MESH)

    kv = jnp.where(c == 0, wk[:, lanes(x // 2 * width, width)], wv[:, lanes(x // 2 * width, width)])
    v.w_all[g, :, width : 2 * width] = wq[...]
    v.w_all[g, :, lanes(c * 2 * width, width)] = kv
    v.wo_all[x, c, g] = wo[...]
    v.tok_all[s] = scaled(tok[...].astype(F32), in_gain[...]).astype(BF16)
    segment = seg[...]
    position = pos[...].astype(F32)
    ends = [
        jnp.sum((segment <= j).astype(F32), axis=1, keepdims=True) for j in range(SEGS)
    ]
    start = jnp.zeros_like(position)
    for end in ends[:-1]:
        start = jnp.maximum(start, jnp.where(position >= end, end, 0.0))
    v.la[...] = jnp.zeros_like(v.la)

    def bounds(size):
        line = lax.broadcasted_iota(jnp.int32, (16, size), 0)
        first, last = jnp.zeros((16, size), F32), jnp.full((16, size), -1.0, F32)
        for j in range(SEGS):
            last = jnp.where(line == j, ends[j] - 1.0, last)
            if j > 0:
                first = jnp.where(line == j, ends[j - 1], first)
        return first, last

    def rope_tables():
        for n in range(pack // 128):
            block = slice(n * 128, (n + 1) * 128)
            pos_col, start_col = column(position[:, block]), column(start[:, block])
            v.pos_col[block], v.start_col[block] = pos_col, start_col
            angle = (pos_col - start_col) * freq[...]
            v.cos[block], v.sin[block] = jnp.cos(angle), jnp.sin(angle)
            yield

    pl.semaphore_wait(entry, len(peers))

    block = lambda g: v.w_all.at[g, :, lanes(c * width, 2 * width)]
    plane = lambda c: lambda z: v.w_all.at[pl.ds(z * NY, NY), :, lanes(c * 2 * width, width)]
    wo_block = lambda n: lambda g: v.wo_all.at[n, c, g]
    wo_plane = lambda n, c: lambda z: v.wo_all.at[n, c, pl.ds(z * NY, NY)]

    def flow(n, way):
        return way(place, link, wo_block(n), wo_plane(n, c), wo_plane(n, 1 - c), d.wo[n])

    weights = gather_zy(place, link, block, plane(c), plane(1 - c), d.w)
    tokens = gather_rows(place, link, v.tok_all, d.ts, d.tr)
    background = together([
        flow(2, gather_zy), flow(3, gather_zy), flow(0, gather_yz), flow(1, gather_yz)
    ])
    tables = rope_tables()
    own = v.wo_all.at[x, c, g]
    for n, way in enumerate((1, -1, 2)):
        link.send(own, own, d.xs.at[n], d.xr.at[n], place.xn(way))
    for t in range(nz // 2 + 4):
        pump(weights, 1)
        if t in (0, 3, 4, 5, 6) or t >= 7:
            pump(tokens, 1)
        if t == 0:
            _, last = bounds(rows)
            select = (last == pos[:, lanes(s * rows, rows)].astype(F32)).astype(BF16)
            found = jnp.dot(select, tok[...], preferred_element_type=F32).astype(BF16)
            for n in range(NS):
                v.tl_out[n] = found[:, n * width : (n + 1) * width]
            v.tl_in[s] = v.tl_out[s]
            for n in range(1, NS):
                to = (s + n) % NS
                link.send(v.tl_out.at[to], v.tl_in.at[s], d.s1.at[n], d.r1.at[n], {"seq": to})
        if t == 1:
            for n, way in enumerate((1, -1, 2)):
                link.arrived(v.wo_all.at[(x - way + NX) % NX, c, g], d.xs.at[0], d.xr.at[n])
        if t >= 1:
            pump(background, 1)
        pump(tables, 1)
    for _ in together([weights, tokens, tables]):
        pass

    pump(background, 1)
    rest = v.w_all[...].reshape(model, 3 * width)
    part = 4
    for n in range(NS // part):
        here = slice(n * part * rows, (n + 1) * part * rows)
        raw = jnp.dot(
            v.tok_all[n * part : (n + 1) * part].reshape(part * rows, model),
            rest,
            preferred_element_type=F32,
        )
        cosine, sine = v.cos[here], v.sin[here]
        key = rotated(scaled(raw[:, :width], k_gain[...]), cosine, sine)
        query = rotated(scaled(raw[:, width : 2 * width], q_gain[...]), cosine, sine)
        v.query[here] = query.astype(BF16)
        v.kv[here, :width] = key.astype(BF16)
        v.kv[here, width:] = scaled(raw[:, 2 * width :], None).astype(BF16)
        pump(background, 1)

    first, last = bounds(pack)
    select = (last == position).astype(BF16)
    query = jnp.dot(select, v.query[...], preferred_element_type=F32).astype(BF16)
    masked = jnp.where(
        (position <= last) & (position >= first), nt(query, v.kv[:, :width]), -1e30
    )
    raw = jnp.exp(masked - jnp.max(masked, axis=1, keepdims=True))
    weights = (raw / jnp.sum(raw, axis=1, keepdims=True)).astype(BF16)
    attended = jnp.dot(weights, v.kv[:, width:], preferred_element_type=F32)
    v.la[s, 0:16] = attended.astype(BF16)
    mine = v.la.at[s, pl.ds(0, 16)]
    for n in range(1, NS):
        link.send(mine, mine, d.ls.at[n], d.lr.at[n], place.sn(n))
    for _ in background:
        pass
    for n in range(1, NS):
        link.arrived(v.la.at[(s - n + NS) % NS, pl.ds(0, 16)], d.ls.at[0], d.lr.at[n])
        link.arrived(v.tl_in.at[(s - n + NS) % NS], d.s1.at[0], d.r1.at[n])

    span = 512
    depth = wo.shape[0]

    def project(source):
        for m in range(model // span):
            total = jnp.zeros((span, rows), F32)
            for n in range(NS):
                w = v.wo_all[n // 2, n % 2, m * span // depth : (m + 1) * span // depth]
                total = total + nt(w.reshape(span, width), source[n]).astype(BF16).astype(F32)
            for n in range(span // 128):
                v.summed[:, m * span + n * 128 : m * span + (n + 1) * 128] = total[
                    n * 128 : (n + 1) * 128
                ].T

    project(v.la)
    total = v.summed[0:16]
    scale = lax.rsqrt(jnp.mean(total * total, axis=1, keepdims=True) + eps)
    here = lanes(s * width, width)
    total = v.summed[0:16, here] * scale * post_gain[:, here]
    states = (jnp.sum(v.tl_in[...].astype(F32), axis=0) + total).astype(BF16).astype(F32)
    v.zbuf[z] = states[:SEGS]
    for n in range(1, nz):
        link.send(v.zbuf.at[z], v.zbuf.at[z], d.s2.at[n], d.r2.at[n], place.zn(n))

    for n, way in enumerate((2, 1, -1, 0)):
        chip = (x + way + NX) % NX
        here = pl.ds(pl.multiple_of(chip * 2 * rows, 256), 2 * rows)
        scores = nt(v.query[here], v.kv[:, :width])
        allowed = (position <= v.pos_col[here, 0:1]) & (position >= v.start_col[here, 0:1])
        masked = jnp.where(allowed, scores, -1e30)
        raw = jnp.exp(masked - jnp.max(masked, axis=1, keepdims=True))
        weights = (raw / jnp.sum(raw, axis=1, keepdims=True)).astype(BF16)
        attended = jnp.dot(weights, v.kv[:, width:], preferred_element_type=F32).astype(BF16)
        v.att[2 * chip] = attended[:rows]
        v.att[2 * chip + 1] = attended[rows:]
        there = 2 * chip + 1 - c
        link.send(v.att.at[there], v.att_in.at[s], d.asend.at[n, 0], d.arecv.at[n, 0], {"seq": there})
        if way == 0:
            v.att_in[s] = v.att[s]
        else:
            there = 2 * chip + c
            link.send(
                v.att.at[there], v.att_in.at[s], d.asend.at[n, 1], d.arecv.at[n, 1], {"seq": there}
            )

    for n in range(1, nz):
        link.arrived(v.zbuf.at[(z - n + nz) % nz], d.s2.at[0], d.r2.at[n])
    for n in range(nz):
        v.rows[n * SEGS : (n + 1) * SEGS] = v.zbuf[n]
    v.buf[s, y] = v.rows[...].astype(BF16)
    for n in range(1, NY):
        link.send(v.buf.at[s, y], v.buf.at[s, y], d.s3.at[n], d.r3.at[n], place.yn(n))

    table = column(pages[...].astype(F32))
    whole, within = pos[...] // PAGE_SLOTS, pos[...] % PAGE_SLOTS
    count = pages.shape[1]
    match = lax.broadcasted_iota(jnp.int32, (count, pack), 0) == whole
    page = jnp.sum(jnp.where(match, table[:, 0:1], 0.0), axis=0, keepdims=True)
    physical = page.astype(jnp.int32) * PAGE_SLOTS + within
    slot = lax.broadcasted_iota(jnp.int32, (rows, pack), 0)
    partner = (s + NS // 2) % NS
    for n, owner in enumerate((partner, s)):
        pick = (slot + owner * rows == physical).astype(BF16)
        picked = jnp.dot(pick, v.kv[...], preferred_element_type=F32).astype(BF16)
        if n == 0:
            v.kv_out[...] = picked
            link.send(v.kv_out, v.kv_in, d.ks, d.kr, {"seq": partner})
        else:
            mine = x // 2 * width
            cache_out[:, lanes(mine, width)] = picked[:, :width]
            cache_out[:, lanes(KEY_HEADS * width + mine, width)] = picked[:, width:]

    for n in range(1, NY):
        link.arrived(v.buf.at[s, (y - n + NY) % NY], d.s3.at[0], d.r3.at[n])
    for n in range(1, NX):
        link.send(v.buf.at[s], v.buf.at[s], d.s4.at[n], d.r4.at[n], place.xn(n))
    link.send(v.buf.at[s], v.buf.at[s], d.s4.at[0], d.r4.at[0], place.sib)

    for n, way in enumerate((2, 1, -1, 0)):
        chip = (x - way + NX) % NX
        link.arrived(v.att_in.at[2 * chip + 1 - c], d.asend.at[0, 0], d.arecv.at[n, 0])
        if way != 0:
            link.arrived(v.att_in.at[2 * chip + c], d.asend.at[0, 0], d.arecv.at[n, 1])
    project(v.att_in)
    hidden = tok[...].astype(F32) + scaled(v.summed[...], post_gain[...])
    hidden_out[...] = hidden.astype(BF16)
    link.arrived(v.kv_in, d.ks, d.kr)
    other = (1 - x // 2) * width
    cache_out[:, lanes(other, width)] = v.kv_in[:, :width]
    cache_out[:, lanes(KEY_HEADS * width + other, width)] = v.kv_in[:, width:]

    for n in (1, 3, 2):
        came = v.buf.at[place.xs(-n)]
        link.arrived(came, d.s4.at[0], d.r4.at[n])
        link.send(came, came, d.s5.at[n], d.r5.at[n], place.sib)
    for n in range(NX):
        came = v.buf.at[2 * ((x - n + NX) % NX) + 1 - c]
        link.arrived(came, d.s4.at[0], d.r4.at[0] if n == 0 else d.r5.at[n])
    count = NY * nz * SEGS
    total = jnp.zeros((count, 1), F32)
    for n in range(NS):
        value = v.buf[n].reshape(count, width).astype(F32)
        total = total + jnp.sum(value * value, axis=1, keepdims=True)
    mean = total / model
    norm_row = jnp.broadcast_to(jnp.sqrt(mean), (count, 128)).T[:8]
    scale = lax.rsqrt(mean + eps)
    fetch.wait()
    logits = jnp.zeros((v.emb.shape[0], count), F32)
    for n in range(NS):
        value = v.buf[n].reshape(count, width).astype(F32)
        final = (value * scale * final_gain[:, n * width : (n + 1) * width]).astype(BF16)
        logits = logits + nt(v.emb[:, n * width : (n + 1) * width], final)
    near = [(a, b) for a in range(NY) for b in range(NS)]
    v.m1[y * NS + s] = jnp.max(logits, axis=0, keepdims=True)
    for n, (a, b) in enumerate(near[1:], 1):
        to = {"grp": z * NY + (y + a) % NY, "seq": (s + b) % NS}
        link.send(v.m1.at[y * NS + s], v.m1.at[y * NS + s], d.s6.at[n], d.r6.at[n], to)
    for n, (a, b) in enumerate(near[1:], 1):
        slot = (y - a + NY) % NY * NS + (s - b + NS) % NS
        link.arrived(v.m1.at[slot], d.s6.at[0], d.r6.at[n])
    v.m3[z] = jnp.max(v.m1[...], axis=0)
    for n in range(1, nz):
        link.send(v.m3.at[z], v.m3.at[z], d.s8.at[n], d.r8.at[n], place.zn(n))
    for n in range(1, nz):
        link.arrived(v.m3.at[(z - n + nz) % nz], d.s8.at[0], d.r8.at[n])
    top = cap_value * jnp.tanh(jnp.max(v.m3[...], axis=0) / cap_value)
    both = jnp.where(lax.broadcasted_iota(jnp.int32, (8, count), 0) == 0, top, norm_row)
    line = lax.broadcasted_iota(jnp.int32, (count, count), 0)
    place_of = lax.broadcasted_iota(jnp.int32, (count, count), 1)
    line_of = (
        place_of // SEGS % NY * (nz * SEGS) + place_of // (NY * SEGS) * SEGS + place_of % SEGS
    )
    both = jnp.dot(
        both,
        (line == line_of).astype(F32),
        precision=lax.Precision.HIGHEST,
        preferred_element_type=F32,
    )
    max_out[...] = both[0:1]
    norm_out[...] = both[1:2]
    link.finish()


class Named:
    pass


def whole_call(nz, *args):
    tok, _, pos, _, _, freq, wq, wk, wv, wo, q_gain, _, _, _, embed = args
    rows, model = tok.shape
    pack, width = pos.shape[1], q_gain.shape[1]
    grp = nz * NY
    count = grp * SEGS
    ring = lambda: [DMA((nz,)), DMA((nz,)), DMA((3, nz)), DMA((3, nz)), DMA((nz,)), DMA((nz,))]
    plain = lambda: [DMA((nz,)), DMA((nz,)), DMA((3,)), DMA((3,)), DMA((nz,)), DMA((nz,))]
    buffers = dict(
        emb=(embed.shape, BF16),
        tok_all=((NS, rows, model), BF16),
        w_all=((grp, wq.shape[0], 3 * width), BF16),
        wo_all=((NX, 2, grp) + wo.shape, BF16),
        pos_col=((pack, 128), F32),
        start_col=((pack, 128), F32),
        cos=((pack, 128), F32),
        sin=((pack, 128), F32),
        query=((pack, width), BF16),
        kv=((pack, 2 * width), BF16),
        att=((NS, rows, width), BF16),
        att_in=((NS, rows, width), BF16),
        kv_out=((rows, 2 * width), BF16),
        kv_in=((rows, 2 * width), BF16),
        summed=((rows, model), F32),
        la=((NS, rows, width), BF16),
        tl_out=((NS, 16, width), BF16),
        tl_in=((NS, 16, width), BF16),
        zbuf=((nz, SEGS, width), F32),
        rows=((nz * SEGS, width), F32),
        buf=((NS, NY, nz * SEGS, width), BF16),
        m1=((NY * NS, 1, count), F32),
        m3=((nz, 1, count), F32),
    )
    pair = lambda a, b, shape: {a: DMA(shape), b: DMA(shape)}
    sems = dict(fetch=DMA, ts=DMA((7, CHUNKS)), tr=DMA((NS, CHUNKS)), ks=DMA, kr=DMA)
    sems |= pair("xs", "xr", (3,)) | pair("asend", "arecv", (4, 2))
    sems |= pair("s1", "r1", (NS,)) | pair("s2", "r2", (nz,)) | pair("s3", "r3", (NY,))
    sems |= pair("s4", "r4", (NX,)) | pair("s5", "r5", (NX,)) | pair("s6", "r6", (NY * NS,))
    sems |= pair("ls", "lr", (NS,)) | pair("s8", "r8", (nz,))
    flows = [ring(), plain(), plain(), ring(), ring()]
    scratch = (
        [pltpu.VMEM(*b) for b in buffers.values()]
        + list(sems.values())
        + [sem for one in flows for sem in one]
    )

    def kernel(*refs):
        refs, extra = list(refs[:19]), list(refs[19:])
        v, d = Named(), Named()
        for name in buffers:
            setattr(v, name, extra.pop(0))
        for name in sems:
            setattr(d, name, extra.pop(0))
        groups = [tuple(extra[6 * n : 6 * n + 6]) for n in range(len(flows))]
        d.w, d.wo = groups[0], groups[1:]
        whole_kernel(nz, *refs, v, d)

    return pl.pallas_call(
        kernel,
        out_shape=(
            jax.ShapeDtypeStruct((rows, model), BF16),
            jax.ShapeDtypeStruct((rows, 2 * KEY_HEADS * width), BF16),
            jax.ShapeDtypeStruct((1, count), F32),
            jax.ShapeDtypeStruct((1, count), F32),
        ),
        in_specs=[VMEM] * 14 + [ANY],
        out_specs=[VMEM] * 4,
        scratch_shapes=scratch,
        compiler_params=pltpu.CompilerParams(
            collective_id=0, has_side_effects=True, vmem_limit_bytes=56 * 1024 * 1024
        ),
        name="whole",
    )(*args)


def store_kernel(*refs):
    half = len(refs) // 2
    for source, target in zip(refs[:half], refs[half:]):
        target[...] = source[...]


def store_call(*arrays):
    return pl.pallas_call(
        store_kernel,
        out_shape=[jax.ShapeDtypeStruct(a.shape, a.dtype) for a in arrays],
        in_specs=[VMEM] * len(arrays),
        out_specs=[VMEM] * len(arrays),
        name="store",
    )(*arrays)


def shards(
    tokens, seg_ids, deal, page_table, in_gain, w_query, key_weight, value_weight,
    q_gain, key_gain, w_out, post_gain, final_gain, embed,
):
    nz = lax.axis_size("grp") // NY
    half = q_gain.shape[0] // 2
    frequency = rope_base ** (-2.0 * jnp.arange(half, dtype=F32) / q_gain.shape[0])
    hidden, cache, norm, top = whole_call(
        nz, tokens[0], seg_ids, deal, page_table, in_gain[None], frequency[None],
        w_query, key_weight, value_weight, w_out.T, q_gain[None], key_gain[None],
        post_gain[None], final_gain[None], embed,
    )
    hidden, cache, norm, top = store_call(hidden, cache, norm, top)
    pages = cache.shape[0] // PAGE_SLOTS
    cache = cache.reshape(pages, PAGE_SLOTS, cache.shape[1])
    return (hidden[None], cache[None], norm[0], top[0])


def solution(mesh):
    return jax.shard_map(
        shards,
        mesh=mesh,
        in_specs=(
            P("grp", "seq", None),
            P("grp", None),
            P("grp", None),
            P("grp", None),
            P(),
            P("grp", "seq"),
            P("grp", None),
            P("grp", None),
            P(),
            P(),
            P("seq", "grp"),
            P(),
            P(),
            P(("grp", "seq"), None),
        ),
        out_specs=(P("grp", "seq", None), P("grp", "seq", None, None), P(), P()),
        check_vma=False,
    )
```
